512 devices in a mesh: seg: 32 (over y_lo, x, core), head: 16 (over z, y_hi).
Axes of the slice: x: 4, y: 8 (y_hi: 2, y_lo: 4; y = y_hi * 4 + y_lo), z: 8, core: 2. Of those that a mesh axis runs over, the one named last changes fastest.
Arguments:
- attn_query: bfloat16 [8, 4096, 3072], P(None, 'seg', 'head'), may hold values from -8 to 8
- attn_key: bfloat16 [8, 4096, 3072], P(None, 'seg', 'head'), may hold values from -8 to 8
- attn_value: bfloat16 [8, 4096, 3072], P(None, 'seg', 'head'), may hold values from -6 to 6
- prompt_len: int32 [8, 32], P(None, 'seg'), may hold values from 1 to 64, as said below
- ttt_weight: bfloat16 [3072, 9216], P(None, 'head'), may hold values from -0.109375 to 0.109375
- init_w1: float32 [48, 64, 256], P('head'), may hold values from -0.75 to 0.75
- init_w2t: float32 [48, 64, 256], P('head'), may hold values from -0.375 to 0.375
- step_rate: float32 [8, 48, 4096], P(None, 'head', 'seg'), may hold values from 0.005 to 0.05
Outputs:
- ttt_out: bfloat16 [8, 4096, 3072], P(None, 'seg', 'head')
The draws below stay inside these ranges and needn't reach their ends.
Inputs may be any that keep to these rules, and one draw needn't show every extreme that they name: `prompt_len`: some entry equals 64.
All inputs are finite; a program needn't handle non-finite values.
Results may differ from the reference program's by a relative error of at most 0.008.
Values may be sent and summed in bfloat16 or wider, within the bound.
A program may use at most 64 MiB of HBM per device.

```python
import math
import jax
import jax.numpy as jnp
from jax import lax

D = 3072
HEADS = 48
HEAD_DIM = 64
FAST = 256
MINI = 64
TEXT_SLOTS = 64
VIDEOS = 8
SEG_TOK = 128
SEGMENTS = 32
SEQ = 4096


def attention_pair(key):
    key_query, key_key = jax.random.split(jax.random.fold_in(key, 11), 2)
    queries = jnp.clip(jax.random.normal(key_query, (VIDEOS, SEQ, D), jnp.float32), -4.0, 4.0)
    key_rows = jnp.clip(jax.random.normal(key_key, (VIDEOS, SEQ, D), jnp.float32), -4.0, 4.0)
    return (queries, key_rows)


def draw_attn_query(key, part):
    return attention_pair(key)[0].astype(jnp.bfloat16)


def draw_attn_key(key, part):
    return attention_pair(key)[1].astype(jnp.bfloat16)


def draw_prompt_len(key, part):
    key_lengths, key_place = jax.random.split(jax.random.fold_in(key, 23))
    lengths = jax.random.randint(key_lengths, (VIDEOS * SEGMENTS,), 1, TEXT_SLOTS + 1)
    place = jax.random.randint(key_place, (), 0, VIDEOS * SEGMENTS)
    lengths = lengths.at[place].set(TEXT_SLOTS)
    return lengths.reshape(VIDEOS, SEGMENTS).astype(jnp.int32)


def level_of(rng, dims, cuts, low, high):
    gain = 1.0
    for axis_at, shards_of in cuts:
        draws = jax.random.uniform(jax.random.fold_in(jax.random.fold_in(rng, 6), axis_at), (shards_of,), jnp.float32, low / len(cuts), high / len(cuts))
        gain = gain * jnp.repeat(jnp.exp(draws), dims[axis_at] // shards_of).reshape((-1,) + (1,) * (len(dims) - 1 - axis_at))
    return gain


def centred(key, extent, deviation, limit, cuts=(), kind=jnp.bfloat16):
    entries = deviation * jax.random.normal(key, extent, jnp.float32)
    if cuts:
        entries = entries * level_of(key, extent, cuts, -0.22, 0.18)
    return jnp.clip(entries, -limit, limit).astype(kind)


def setup_inputs(seed: int = 0) -> dict:
    key_of = jax.random.split(jax.random.key(seed), 9)
    return {
        "attn_query": draw_attn_query(jax.random.fold_in(key_of[8], 71), 0),
        "attn_key": draw_attn_key(jax.random.fold_in(key_of[8], 71), 0),
        "attn_value": centred(key_of[2], (VIDEOS, SEQ, D), 1.0, 6.0, ((1, 32), (2, 16))),
        "prompt_len": draw_prompt_len(jax.random.fold_in(key_of[8], 71), 0),
        "ttt_weight": centred(key_of[4], (D, 3 * D), D ** -0.5, 0.109375, ((1, 16),)),
        "init_w1": centred(key_of[5], (HEADS, HEAD_DIM, FAST), HEAD_DIM ** -0.5, 0.75, ((0, 16),), jnp.float32),
        "init_w2t": centred(key_of[6], (HEADS, HEAD_DIM, FAST), FAST ** -0.5, 0.375, ((0, 16),), jnp.float32),
        "step_rate": jnp.clip(jnp.exp(math.log(0.05) - 2.3025851 * jax.random.uniform(key_of[7], (VIDEOS, HEADS, SEQ), jnp.float32) ** level_of(key_of[7], (VIDEOS, HEADS, SEQ), ((1, 16), (2, 32)), -0.2, 0.2)), 0.005, 0.05),
    }


highest_precision = lax.Precision.HIGHEST
norm_epsilon = 1e-05
rms_epsilon = 1e-06

def normalize(values):
    center = values - lax.optimization_barrier(jnp.mean(values, axis=-1, keepdims=True))
    spread = lax.optimization_barrier(jnp.mean(center * center, axis=-1, keepdims=True))
    return center * lax.rsqrt(spread + norm_epsilon)

def fast_mlp(inputs, fast_weights):
    hidden = jax.nn.gelu(jnp.einsum('bmd,bdf->bmf', inputs, fast_weights[:, 0], precision=highest_precision), approximate=True)
    return normalize(jnp.einsum('bmf,bdf->bmd', hidden, fast_weights[:, 1], precision=highest_precision))

def minibatch(fast_weights, batch_items):
    queries, key_rows, value_rows, step_rates = batch_items
    target = value_rows - key_rows

    def loss_value(weights_now):
        error = fast_mlp(key_rows, weights_now) - target
        return 0.5 * jnp.sum(step_rates[:, :, None] * error * error) / step_rates.shape[-1]
    gradient = jax.grad(loss_value)(fast_weights)
    fast_weights = fast_weights - gradient
    return (fast_weights, queries + fast_mlp(queries, fast_weights))

def segment_attention(operands):
    query_block, key_block, value_block, length = operands
    position = jnp.arange(SEG_TOK, dtype=jnp.int32)
    usable = (position >= TEXT_SLOTS) | (position < length)
    scores = jnp.einsum('qhd,khd->hqk', query_block.astype(jnp.float32), key_block.astype(jnp.float32)) * HEAD_DIM ** (-0.5)
    scores = jnp.where(usable[None, None, :], scores, -1e+30)
    largest = lax.optimization_barrier(jnp.max(scores, axis=-1, keepdims=True))
    exponent = jnp.exp(scores - largest)
    weights = (exponent / lax.optimization_barrier(jnp.sum(exponent, axis=-1, keepdims=True))).astype(jnp.bfloat16)
    mixed = jnp.einsum('hqk,khd->qhd', weights.astype(jnp.float32), value_block.astype(jnp.float32))
    return mixed.astype(jnp.bfloat16)

def reference(attn_query, attn_key, attn_value, prompt_len, ttt_weight, init_w1, init_w2t, step_rate):
    block_count = VIDEOS * SEGMENTS

    def reshape_blocks(array):
        return array.reshape(block_count, SEG_TOK, HEADS, HEAD_DIM)
    attended = lax.map(segment_attention, (reshape_blocks(attn_query), reshape_blocks(attn_key), reshape_blocks(attn_value), prompt_len.reshape(block_count)))
    features = attended.reshape(VIDEOS * SEQ, D).astype(jnp.float32)
    normed = (features * lax.rsqrt(lax.optimization_barrier(jnp.mean(features * features, axis=-1, keepdims=True)) + rms_epsilon)).astype(jnp.bfloat16)
    projected = jnp.dot(normed, ttt_weight, preferred_element_type=jnp.float32)
    projected = projected.reshape(VIDEOS, SEQ, HEADS, 3, HEAD_DIM).transpose(0, 2, 3, 1, 4)
    step_count = SEQ // MINI

    def to_blocks(array):
        return array.reshape(VIDEOS * HEADS, step_count, MINI, HEAD_DIM).transpose(1, 0, 2, 3)
    position = jnp.arange(SEQ, dtype=jnp.int32)
    within = position % SEG_TOK
    segment = position // SEG_TOK
    lengths = prompt_len[:, segment]
    usable = (within >= TEXT_SLOTS)[None, :] | (within[None, :] < lengths)
    step_rates = step_rate * usable[:, None, :].astype(jnp.float32)
    rate_blocks = step_rates.reshape(VIDEOS * HEADS, step_count, MINI).transpose(1, 0, 2)
    start = jnp.stack([init_w1, init_w2t], axis=1)
    start = jnp.broadcast_to(start[None], (VIDEOS,) + start.shape).reshape(VIDEOS * HEADS, 2, HEAD_DIM, FAST)
    final_weights, outputs = lax.scan(minibatch, start, (to_blocks(projected[:, :, 0]), to_blocks(projected[:, :, 1]), to_blocks(projected[:, :, 2]), rate_blocks))
    outputs = outputs.transpose(1, 0, 2, 3).reshape(VIDEOS, HEADS, SEQ, HEAD_DIM).transpose(0, 2, 1, 3)
    return outputs.reshape(VIDEOS, SEQ, D).astype(jnp.bfloat16)
```

```python
import math

import jax
import jax.numpy as jnp
from jax import lax
from jax.experimental import pallas as pl
from jax.experimental.pallas import tpu as pltpu
from jax.sharding import PartitionSpec as P

F32, BF = jnp.float32, jnp.bfloat16
GC = math.sqrt(2.0 / math.pi)
GA = 0.044715
VMEM_SPEC = pl.BlockSpec(memory_space=pltpu.VMEM)


def nn(a, b):
    return lax.dot_general(a, b, (((1,), (0,)), ((), ())), preferred_element_type=F32)


def nt(a, b):
    return lax.dot_general(a, b, (((1,), (1,)), ((), ())), preferred_element_type=F32)


def tn(a, b):
    return lax.dot_general(a, b, (((0,), (0,)), ((), ())), preferred_element_type=F32)


def attend(q, k, v, length, put):
    position = lax.broadcasted_iota(jnp.int32, (128, 1), 0)
    usable = (position >= 64) | (position < length)
    for h in range(3):
        cols = slice(64 * h, 64 * h + 64)
        scores = nt(k[:, cols], q[:, cols]) * 0.125
        scores = jnp.where(usable, scores, -1e30)
        exponent = jnp.exp(scores - jnp.max(scores, axis=0, keepdims=True))
        weights = (exponent * (1.0 / jnp.sum(exponent, axis=0, keepdims=True))).astype(BF)
        put(h, tn(v[:, cols], weights).astype(BF))


def attention_kernel(lengths, q, k, v, out):
    def put(h, value):
        out[0, 64 * h : 64 * h + 64, :] = value

    attend(q[0], k[0], v[0], lengths[pl.program_id(0), 0], put)


def attention(lengths, q, k, v):
    block = pl.BlockSpec((1, 128, 192), lambda i: (i, 0, 0))
    return pl.pallas_call(
        attention_kernel,
        grid=(8,),
        out_shape=jax.ShapeDtypeStruct((8, 192, 128), BF),
        in_specs=[pl.BlockSpec(memory_space=pltpu.SMEM), block, block, block],
        out_specs=pl.BlockSpec((1, 192, 128), lambda i: (i, 0, 0)),
        name="segment_attention",
    )(lengths, q, k, v)


def project_kernel(lengths, a, wt, rate, out):
    pair = pl.program_id(0)
    x = jnp.concatenate(
        [a[:, 0].reshape(3072, 128), a[:, 1].reshape(3072, 128)], axis=1
    ).astype(F32)
    scale = lax.rsqrt(jnp.mean(x * x, axis=0, keepdims=True) + 1e-6)
    normed = (x * scale).astype(BF)
    position = lax.broadcasted_iota(jnp.int32, (1, 128), 1)
    projected = nn(wt[...], normed).astype(BF)
    for half in range(2):
        usable = (position >= 64) | (position < lengths[2 * pair + half, 0])
        for h in range(3):
            item = 3 * half + h
            out[item, 0:192, :] = projected[192 * h : 192 * h + 192, 128 * half : 128 * half + 128]
            eta = jnp.where(usable, rate[half, h : h + 1, :], 0.0)
            out[item, 192:208, :] = jnp.broadcast_to(eta, (16, 128)).astype(BF)


def project(lengths, gathered, wt, rate):
    return pl.pallas_call(
        project_kernel,
        grid=(4,),
        out_shape=jax.ShapeDtypeStruct((24, 208, 128), BF),
        in_specs=[
            pl.BlockSpec(memory_space=pltpu.SMEM),
            pl.BlockSpec((16, 2, 192, 128), lambda i: (0, i, 0, 0)),
            pl.BlockSpec((576, 3072), lambda i: (0, 0)),
            pl.BlockSpec((2, 3, 128), lambda i: (i, 0, 0)),
        ],
        out_specs=pl.BlockSpec((6, 208, 128), lambda i: (i, 0, 0)),
        compiler_params=pltpu.CompilerParams(vmem_limit_bytes=48 << 20),
        name="norm_project",
    )(lengths, gathered, wt, rate)


def forward(u, w2b, xt, st):
    sq = u * u
    t = jnp.tanh(u * (GC + (GC * GA) * sq))
    half = 0.5 + 0.5 * t
    hb = (u * half).astype(BF)
    z = nn(w2b, hb)
    center = z - jnp.mean(z, axis=0, keepdims=True)
    rs = lax.rsqrt(jnp.mean(center * center, axis=0, keepdims=True) + 1e-5)
    y = center * rs
    return sq, t, half, hb, rs, y, y + (xt - st)


def scan_items(get, put, w1t0, w2t0, w2c0, w1s, w2s, w2ts, ub, xs, rprev, count):
    left = lax.broadcasted_iota(jnp.int32, (64, 128), 1) < 64
    left1 = lax.broadcasted_iota(jnp.int32, (1, 128), 1) < 64
    zero = jnp.zeros((64, 128), F32)
    zero1 = jnp.zeros((1, 128), F32)
    w1s[...] = w1t0[...]
    w2s[...] = w2t0[...]
    w2ts[...] = w2c0[...]
    x0 = jnp.where(left, get(0, 64, 64), zero)
    ub[...] = nn(w1s[...].astype(BF), x0.astype(BF))
    xs[...] = x0.T.astype(BF)

    def step(xt, st, eta, xnt):
        xntb = xnt.astype(BF)
        u = ub[...]
        sq, t, half, hb, rs, y, r = forward(u, w2s[...].astype(BF), xt, st)
        dy = r * (eta * (1.0 / 64.0))
        m1 = jnp.mean(dy, axis=0, keepdims=True)
        m2 = jnp.mean(dy * y, axis=0, keepdims=True)
        dzb = (rs * (dy - m1 - y * m2)).astype(BF)
        slope = half + (0.5 * u) * ((1.0 - t * t) * (GC + (3.0 * GC * GA) * sq))
        dub = (nn(w2ts[...].astype(BF), dzb) * slope).astype(BF)
        x = xs[...]
        w1 = w1s[...]
        ub[...] = nn(w1.astype(BF), xntb) - nn(dub, nn(x, xntb).astype(BF))
        w1s[...] = w1 - nn(dub, x)
        w2s[...] -= nt(dzb, hb)
        w2ts[...] -= nt(hb, dzb)
        xs[...] = xnt.T.astype(BF)
        return r

    def segment(s, carry):
        prev = jnp.maximum(s - 1, 0)
        qs, ks, vs = get(s, 0, 64), get(s, 64, 64), get(s, 128, 64)
        qp = get(prev, 0, 64)
        kn = get(jnp.minimum(s + 1, count - 1), 64, 64)
        rate = get(s, 192, 1)
        mid = jnp.where(left, qs, ks)
        even = step(
            jnp.where(left, ks, qp), jnp.where(left, vs, zero), jnp.where(left1, rate, zero1), mid
        )
        put(prev, jnp.where(left, rprev[...], even).astype(BF))
        rprev[...] = step(
            mid, jnp.where(left, zero, vs), jnp.where(left1, zero1, rate), jnp.where(left, kn, qs)
        )
        return carry

    rprev[...] = zero
    lax.fori_loop(0, count, segment, 0)
    last = forward(ub[...], w2s[...].astype(BF), get(count - 1, 0, 64), zero)[-1]
    put(count - 1, jnp.where(left, rprev[...], last).astype(BF))


SCAN_SCRATCH = [
    pltpu.VMEM((256, 64), F32),
    pltpu.VMEM((64, 256), F32),
    pltpu.VMEM((256, 64), F32),
    pltpu.VMEM((256, 128), F32),
    pltpu.VMEM((128, 64), BF),
    pltpu.VMEM((64, 128), F32),
]


def scan_kernel(qkv, w1t0, w2t0, w2c0, out, *scratch):
    def get(s, row, rows):
        return qkv[s, row : row + rows, :].astype(F32)

    def put(s, value):
        out[s] = value

    scan_items(get, put, w1t0, w2t0, w2c0, *scratch, qkv.shape[0])


def run_scan(qkv, w1t, w2t, w2c):
    return pl.pallas_call(
        scan_kernel,
        out_shape=jax.ShapeDtypeStruct((qkv.shape[0], 64, 128), BF),
        in_specs=[VMEM_SPEC] * 4,
        out_specs=VMEM_SPEC,
        scratch_shapes=SCAN_SCRATCH,
        name="ttt_scan",
    )(qkv, w1t, w2t, w2c)


def body(attn_query, attn_key, attn_value, prompt_len, ttt_weight, init_w1, init_w2t, step_rate):
    attended = attention(prompt_len, attn_query, attn_key, attn_value)
    gathered = lax.all_gather(attended, "head", axis=0)
    items = project(prompt_len, gathered, ttt_weight.T, step_rate)
    seg_count = lax.axis_size("seg")
    items = jnp.pad(items, ((0, seg_count - items.shape[0]), (0, 0), (0, 0)))
    sequence = lax.all_to_all(items, "seg", 0, 0, tiled=True)
    head = lax.axis_index("seg") % 3
    w1 = lax.dynamic_index_in_dim(init_w1, head, 0, keepdims=False)
    w2t = lax.dynamic_index_in_dim(init_w2t, head, 0, keepdims=False)
    outputs = run_scan(sequence, w1.T, w2t, w2t.T)
    returned = lax.all_to_all(outputs, "seg", 0, 0, tiled=True)
    returned = returned[:24].reshape(8, 192, 128)
    return jnp.swapaxes(returned, 1, 2)


def solution(mesh):
    in_specs = (
        P(None, "seg", "head"),
        P(None, "seg", "head"),
        P(None, "seg", "head"),
        P(None, "seg"),
        P(None, "head"),
        P("head", None, None),
        P("head", None, None),
        P(None, "head", "seg"),
    )
    return jax.shard_map(
        body, mesh=mesh, in_specs=in_specs, out_specs=P(None, "seg", "head"), check_vma=False
    )
```

```python
import math

import jax
import jax.numpy as jnp
from jax import lax
from jax.experimental import pallas as pl
from jax.experimental.pallas import tpu as pltpu
from jax.sharding import PartitionSpec as P

F32, BF = jnp.float32, jnp.bfloat16
GC = math.sqrt(2.0 / math.pi)
GA = 0.044715
MESH = pl.DeviceIdType.MESH
VMEM_SPEC = pl.BlockSpec(memory_space=pltpu.VMEM)


def nn(a, b):
    return lax.dot_general(a, b, (((1,), (0,)), ((), ())), preferred_element_type=F32)


def nt(a, b):
    return lax.dot_general(a, b, (((1,), (1,)), ((), ())), preferred_element_type=F32)


def tn(a, b):
    return lax.dot_general(a, b, (((0,), (0,)), ((), ())), preferred_element_type=F32)


def attend(q, k, v, length, put):
    position = lax.broadcasted_iota(jnp.int32, (128, 1), 0)
    usable = (position >= 64) | (position < length)
    for h in range(3):
        rows = slice(64 * h, 64 * h + 64)
        scores = tn(k[rows, :], q[rows, :]) * 0.125
        scores = jnp.where(usable, scores, -1e30)
        exponent = jnp.exp(scores - jnp.max(scores, axis=0, keepdims=True))
        weights = (exponent * (1.0 / jnp.sum(exponent, axis=0, keepdims=True))).astype(BF)
        put(h, nn(v[rows, :], weights).astype(BF))


def gather_kernel(
    lengths, q, k, v, wt, rate, out, buf, acc, ssq, wv, wsem, psem, rsem, lsem, recv
):
    me = lax.axis_index("head")
    z, y = me // 2, lax.rem(me, 2)
    right, left, partner = lax.rem(me + 2, 16), lax.rem(me + 14, 16), 2 * z + 1 - y
    barrier = pltpu.get_barrier_semaphore()
    for peer in (right, left, partner):
        pl.semaphore_signal(barrier, inc=1, device_id={"head": peer}, device_id_type=MESH)
    pl.semaphore_wait(barrier, 3)
    load = pltpu.make_async_copy(wt, wv, wsem)
    load.start()

    def copy(zo, c, yo, sem, peer):
        return pltpu.make_async_remote_copy(
            src_ref=buf.at[zo, c, yo],
            dst_ref=buf.at[zo, c, yo],
            send_sem=sem,
            recv_sem=recv.at[zo, c, yo],
            device_id={"head": peer},
            device_id_type=MESH,
        )

    def to_right(zo, c, yo, d, o):
        return copy(zo, c, yo, rsem.at[d, o, c], right)

    def to_left(zo, c, yo, d, o):
        return copy(zo, c, yo, lsem.at[d, o, c], left)

    def send_own(c):
        to_right(z, c, y, 0, 0).start()
        to_left(z, c, y, 0, 0).start()
        copy(z, c, y, psem.at[c], partner).start()

    def attend_pair(c, carry):
        for half in range(2):
            video = 2 * c + half

            def put(h, value):
                buf[z, c, y, 64 * h : 64 * h + 64, 128 * half : 128 * half + 128] = value

            attend(q[video], k[video], v[video], lengths[video, 0], put)

        @pl.when(c > 0)
        def _():
            send_own(c - 1)

        return carry

    lax.fori_loop(0, 4, attend_pair, 0)
    load.wait()

    def add(zo, c):
        x = buf[zo, c].reshape(384, 256)
        w = wv[:, pl.ds(pl.multiple_of(zo * 384, 128), 384)]
        acc[c] += nn(w, x)
        xf = x.astype(F32)
        ssq[c] += jnp.sum((xf * xf).reshape(48, 8, 256), axis=0)

    def first(c, carry):
        acc[c] = jnp.zeros((576, 256), F32)
        ssq[c] = jnp.zeros((8, 256), F32)
        copy(z, c, 1 - y, psem.at[c], partner).wait_recv()
        to_right(z, c, 1 - y, 0, 1).start()
        to_left(z, c, 1 - y, 0, 1).start()

        @pl.when(c == 0)
        def _():
            send_own(3)

        add(z, c)
        return carry

    lax.fori_loop(0, 4, first, 0)

    def hop(d, carry):
        zr, zl = lax.rem(z + 8 - d, 8), lax.rem(z + d, 8)
        for o in range(2):
            yo = y if o == 0 else 1 - y

            def chunk(c, inner):
                @pl.when((d < 4) | (c < 2))
                def _():
                    to_right(zr, c, yo, 0, 0).wait_recv()

                @pl.when((d < 3) | ((d == 3) & (c < 2)))
                def _():
                    to_right(zr, c, yo, d, o).start()

                @pl.when((d < 4) | (c >= 2))
                def _():
                    to_left(zl, c, yo, 0, 0).wait_recv()

                @pl.when((d < 3) | ((d == 3) & (c >= 2)))
                def _():
                    to_left(zl, c, yo, d, o).start()

                if o == 1:
                    add(zl, c)

                    @pl.when(d < 4)
                    def _():
                        add(zr, c)

                return inner

            lax.fori_loop(0, 4, chunk, 0)
        return carry

    lax.fori_loop(1, 5, hop, 0)

    position = lax.broadcasted_iota(jnp.int32, (1, 128), 1)

    def finish(c, carry):
        mean = jnp.sum(ssq[c], axis=0, keepdims=True) * (1.0 / 3072.0)
        projected = (acc[c] * lax.rsqrt(mean + 1e-6)).astype(BF)
        for half in range(2):
            video = 2 * c + half
            usable = (position >= 64) | (position < lengths[video, 0])
            for h in range(3):
                item = video * 3 + h
                out[item, 0:192, :] = projected[
                    192 * h : 192 * h + 192, 128 * half : 128 * half + 128
                ]
                eta = jnp.where(usable, rate[h, pl.ds(video, 1), :], 0.0)
                out[item, 192:208, :] = jnp.broadcast_to(eta, (16, 128)).astype(BF)
        copy(z, c, y, psem.at[c], partner).wait_send()
        for o in range(2):
            for d in range(3):
                to_right(z, c, y, d, o).wait_send()
                to_left(z, c, y, d, o).wait_send()

            @pl.when(c < 2)
            def _():
                to_right(z, c, y, 3, o).wait_send()

            @pl.when(c >= 2)
            def _():
                to_left(z, c, y, 3, o).wait_send()

        return carry

    lax.fori_loop(0, 4, finish, 0)


def gather_project(lengths, q, k, v, wt, rate):
    return pl.pallas_call(
        gather_kernel,
        out_shape=jax.ShapeDtypeStruct((24, 208, 128), BF),
        in_specs=[
            pl.BlockSpec(memory_space=pltpu.SMEM),
            VMEM_SPEC,
            VMEM_SPEC,
            VMEM_SPEC,
            pl.BlockSpec(memory_space=pl.ANY),
            VMEM_SPEC,
        ],
        out_specs=VMEM_SPEC,
        scratch_shapes=[
            pltpu.VMEM((8, 4, 2, 192, 256), BF),
            pltpu.VMEM((4, 576, 256), F32),
            pltpu.VMEM((4, 8, 256), F32),
            pltpu.VMEM((576, 3072), BF),
            pltpu.SemaphoreType.DMA,
            pltpu.SemaphoreType.DMA((4,)),
            pltpu.SemaphoreType.DMA((4, 2, 4)),
            pltpu.SemaphoreType.DMA((4, 2, 4)),
            pltpu.SemaphoreType.DMA((8, 4, 2)),
        ],
        compiler_params=pltpu.CompilerParams(
            collective_id=0, has_side_effects=True, vmem_limit_bytes=56 << 20
        ),
        name="attend_gather_project",
    )(lengths, q, k, v, wt, rate)


def forward(u, w2b, xt, st):
    sq = u * u
    t = jnp.tanh(u * (GC + (GC * GA) * sq))
    half = 0.5 + 0.5 * t
    hb = (u * half).astype(BF)
    z = nn(w2b, hb)
    center = z - jnp.mean(z, axis=0, keepdims=True)
    rs = lax.rsqrt(jnp.mean(center * center, axis=0, keepdims=True) + 1e-5)
    y = center * rs
    return sq, t, half, hb, rs, y, y + (xt - st)


def scan_items(get, put, w1t0, w2t0, w2c0, w1s, w2s, w2ts, ub, xs, rprev, count):
    left = lax.broadcasted_iota(jnp.int32, (64, 128), 1) < 64
    left1 = lax.broadcasted_iota(jnp.int32, (1, 128), 1) < 64
    zero = jnp.zeros((64, 128), F32)
    zero1 = jnp.zeros((1, 128), F32)
    w1s[...] = w1t0[...]
    w2s[...] = w2t0[...]
    w2ts[...] = w2c0[...]
    x0 = jnp.where(left, get(0, 64, 64), zero)
    ub[...] = nn(w1s[...].astype(BF), x0.astype(BF))
    xs[...] = x0.T.astype(BF)

    def step(xt, st, eta, xnt):
        xntb = xnt.astype(BF)
        u = ub[...]
        sq, t, half, hb, rs, y, r = forward(u, w2s[...].astype(BF), xt, st)
        dy = r * (eta * (1.0 / 64.0))
        m1 = jnp.mean(dy, axis=0, keepdims=True)
        m2 = jnp.mean(dy * y, axis=0, keepdims=True)
        dzb = (rs * (dy - m1 - y * m2)).astype(BF)
        slope = half + (0.5 * u) * ((1.0 - t * t) * (GC + (3.0 * GC * GA) * sq))
        dub = (nn(w2ts[...].astype(BF), dzb) * slope).astype(BF)
        x = xs[...]
        w1 = w1s[...]
        ub[...] = nn(w1.astype(BF), xntb) - nn(dub, nn(x, xntb).astype(BF))
        w1s[...] = w1 - nn(dub, x)
        w2s[...] -= nt(dzb, hb)
        w2ts[...] -= nt(hb, dzb)
        xs[...] = xnt.T.astype(BF)
        return r

    def segment(s, carry):
        prev = jnp.maximum(s - 1, 0)
        qs, ks, vs = get(s, 0, 64), get(s, 64, 64), get(s, 128, 64)
        qp = get(prev, 0, 64)
        kn = get(jnp.minimum(s + 1, count - 1), 64, 64)
        rate = get(s, 192, 1)
        mid = jnp.where(left, qs, ks)
        even = step(
            jnp.where(left, ks, qp), jnp.where(left, vs, zero), jnp.where(left1, rate, zero1), mid
        )
        put(prev, jnp.where(left, rprev[...], even).astype(BF))
        rprev[...] = step(
            mid, jnp.where(left, zero, vs), jnp.where(left1, zero1, rate), jnp.where(left, kn, qs)
        )
        return carry

    rprev[...] = zero
    lax.fori_loop(0, count, segment, 0)
    last = forward(ub[...], w2s[...].astype(BF), get(count - 1, 0, 64), zero)[-1]
    put(count - 1, jnp.where(left, rprev[...], last).astype(BF))


SCAN_SCRATCH = [
    pltpu.VMEM((256, 64), F32),
    pltpu.VMEM((64, 256), F32),
    pltpu.VMEM((256, 64), F32),
    pltpu.VMEM((256, 128), F32),
    pltpu.VMEM((128, 64), BF),
    pltpu.VMEM((64, 128), F32),
]


def scan_kernel(qkv, w1t0, w2t0, w2c0, out, *scratch):
    def get(s, row, rows):
        return qkv[s, row : row + rows, :].astype(F32)

    def put(s, value):
        out[s] = value

    scan_items(get, put, w1t0, w2t0, w2c0, *scratch, qkv.shape[0])


def run_scan(qkv, w1t, w2t, w2c):
    return pl.pallas_call(
        scan_kernel,
        out_shape=jax.ShapeDtypeStruct((qkv.shape[0], 64, 128), BF),
        in_specs=[VMEM_SPEC] * 4,
        out_specs=VMEM_SPEC,
        scratch_shapes=SCAN_SCRATCH,
        name="ttt_scan",
    )(qkv, w1t, w2t, w2c)


def body(attn_query, attn_key, attn_value, prompt_len, ttt_weight, init_w1, init_w2t, step_rate):
    def turned(array):
        return jnp.swapaxes(array, 1, 2)

    items = gather_project(
        prompt_len,
        turned(attn_query),
        turned(attn_key),
        turned(attn_value),
        ttt_weight.T,
        jnp.swapaxes(step_rate, 0, 1),
    )
    seg_count = lax.axis_size("seg")
    items = jnp.pad(items, ((0, seg_count - items.shape[0]), (0, 0), (0, 0)))
    sequence = lax.all_to_all(items, "seg", 0, 0, tiled=True)
    head = lax.axis_index("seg") % 3
    w1 = lax.dynamic_index_in_dim(init_w1, head, 0, keepdims=False)
    w2t = lax.dynamic_index_in_dim(init_w2t, head, 0, keepdims=False)
    outputs = run_scan(sequence, w1.T, w2t, w2t.T)
    returned = lax.all_to_all(outputs, "seg", 0, 0, tiled=True)
    returned = returned[:24].reshape(8, 192, 128)
    return jnp.swapaxes(returned, 1, 2)


def solution(mesh):
    in_specs = (
        P(None, "seg", "head"),
        P(None, "seg", "head"),
        P(None, "seg", "head"),
        P(None, "seg"),
        P(None, "head"),
        P("head", None, None),
        P("head", None, None),
        P(None, "head", "seg"),
    )
    return jax.shard_map(
        body, mesh=mesh, in_specs=in_specs, out_specs=P(None, "seg", "head"), check_vma=False
    )
```

```python
import math

import jax
import jax.numpy as jnp
from jax import lax
from jax.experimental import pallas as pl
from jax.experimental.pallas import tpu as pltpu
from jax.sharding import PartitionSpec as P

F32, BF = jnp.float32, jnp.bfloat16
GC = math.sqrt(2.0 / math.pi)
GA = 0.044715
MESH = pl.DeviceIdType.MESH
VMEM_SPEC = pl.BlockSpec(memory_space=pltpu.VMEM)


def nn(a, b):
    return lax.dot_general(a, b, (((1,), (0,)), ((), ())), preferred_element_type=F32)


def nt(a, b):
    return lax.dot_general(a, b, (((1,), (1,)), ((), ())), preferred_element_type=F32)


def tn(a, b):
    return lax.dot_general(a, b, (((0,), (0,)), ((), ())), preferred_element_type=F32)


def attend(q, k, v, length, put):
    position = lax.broadcasted_iota(jnp.int32, (128, 1), 0)
    usable = (position >= 64) | (position < length)
    for h in range(3):
        rows = slice(64 * h, 64 * h + 64)
        scores = tn(k[rows, :], q[rows, :]) * 0.125
        scores = jnp.where(usable, scores, -1e30)
        exponent = jnp.exp(scores - jnp.max(scores, axis=0, keepdims=True))
        weights = (exponent * (1.0 / jnp.sum(exponent, axis=0, keepdims=True))).astype(BF)
        put(h, nn(v[rows, :], weights).astype(BF))


def gather_kernel(
    lengths, q, k, v, wt, rate, out, buf, acc, ssq, wv, wsem, psem, rsem, lsem, recv
):
    me = lax.axis_index("head")
    z, y = me // 2, lax.rem(me, 2)
    right, left, partner = lax.rem(me + 2, 16), lax.rem(me + 14, 16), 2 * z + 1 - y
    barrier = pltpu.get_barrier_semaphore()
    for peer in (right, left, partner):
        pl.semaphore_signal(barrier, inc=1, device_id={"head": peer}, device_id_type=MESH)
    pl.semaphore_wait(barrier, 3)
    load = pltpu.make_async_copy(wt, wv, wsem)
    load.start()

    def copy(zo, c, yo, sem, peer):
        return pltpu.make_async_remote_copy(
            src_ref=buf.at[zo, c, yo],
            dst_ref=buf.at[zo, c, yo],
            send_sem=sem,
            recv_sem=recv.at[zo, c, yo],
            device_id={"head": peer},
            device_id_type=MESH,
        )

    def to_right(zo, c, yo, d, o):
        return copy(zo, c, yo, rsem.at[d, o, c], right)

    def to_left(zo, c, yo, d, o):
        return copy(zo, c, yo, lsem.at[d, o, c], left)

    def send_own(c):
        to_right(z, c, y, 0, 0).start()
        to_left(z, c, y, 0, 0).start()
        copy(z, c, y, psem.at[c], partner).start()

    def attend_pair(c, carry):
        for half in range(2):
            video = 2 * c + half

            def put(h, value):
                buf[z, c, y, 64 * h : 64 * h + 64, 128 * half : 128 * half + 128] = value

            attend(q[video], k[video], v[video], lengths[video, 0], put)

        @pl.when(c > 0)
        def _():
            send_own(c - 1)

        return carry

    lax.fori_loop(0, 4, attend_pair, 0)
    load.wait()

    def add(zo, c):
        x = buf[zo, c].reshape(384, 256)
        w = wv[:, pl.ds(pl.multiple_of(zo * 384, 128), 384)]
        acc[c] += nn(w, x)
        xf = x.astype(F32)
        ssq[c] += jnp.sum((xf * xf).reshape(48, 8, 256), axis=0)

    def first(c, carry):
        acc[c] = jnp.zeros((576, 256), F32)
        ssq[c] = jnp.zeros((8, 256), F32)
        copy(z, c, 1 - y, psem.at[c], partner).wait_recv()
        to_right(z, c, 1 - y, 0, 1).start()
        to_left(z, c, 1 - y, 0, 1).start()

        @pl.when(c == 0)
        def _():
            send_own(3)

        add(z, c)
        return carry

    lax.fori_loop(0, 4, first, 0)

    def hop(d, carry):
        zr, zl = lax.rem(z + 8 - d, 8), lax.rem(z + d, 8)
        for o in range(2):
            yo = y if o == 0 else 1 - y

            def chunk(c, inner):
                @pl.when((d < 4) | (c < 2))
                def _():
                    to_right(zr, c, yo, 0, 0).wait_recv()

                @pl.when((d < 3) | ((d == 3) & (c < 2)))
                def _():
                    to_right(zr, c, yo, d, o).start()

                @pl.when((d < 4) | (c >= 2))
                def _():
                    to_left(zl, c, yo, 0, 0).wait_recv()

                @pl.when((d < 3) | ((d == 3) & (c >= 2)))
                def _():
                    to_left(zl, c, yo, d, o).start()

                if o == 1:
                    add(zl, c)

                    @pl.when(d < 4)
                    def _():
                        add(zr, c)

                return inner

            lax.fori_loop(0, 4, chunk, 0)
        return carry

    lax.fori_loop(1, 5, hop, 0)

    position = lax.broadcasted_iota(jnp.int32, (1, 128), 1)

    def finish(c, carry):
        mean = jnp.sum(ssq[c], axis=0, keepdims=True) * (1.0 / 3072.0)
        projected = (acc[c] * lax.rsqrt(mean + 1e-6)).astype(BF)
        for half in range(2):
            video = 2 * c + half
            usable = (position >= 64) | (position < lengths[video, 0])
            for h in range(3):
                item = video * 3 + h
                out[item, 0:192, :] = projected[
                    192 * h : 192 * h + 192, 128 * half : 128 * half + 128
                ]
                eta = jnp.where(usable, rate[h, pl.ds(video, 1), :], 0.0)
                out[item, 192:208, :] = jnp.broadcast_to(eta, (16, 128)).astype(BF)
        copy(z, c, y, psem.at[c], partner).wait_send()
        for o in range(2):
            for d in range(3):
                to_right(z, c, y, d, o).wait_send()
                to_left(z, c, y, d, o).wait_send()

            @pl.when(c < 2)
            def _():
                to_right(z, c, y, 3, o).wait_send()

            @pl.when(c >= 2)
            def _():
                to_left(z, c, y, 3, o).wait_send()

        return carry

    lax.fori_loop(0, 4, finish, 0)


def gather_project(lengths, q, k, v, wt, rate):
    return pl.pallas_call(
        gather_kernel,
        out_shape=jax.ShapeDtypeStruct((24, 208, 128), BF),
        in_specs=[
            pl.BlockSpec(memory_space=pltpu.SMEM),
            VMEM_SPEC,
            VMEM_SPEC,
            VMEM_SPEC,
            pl.BlockSpec(memory_space=pl.ANY),
            VMEM_SPEC,
        ],
        out_specs=VMEM_SPEC,
        scratch_shapes=[
            pltpu.VMEM((8, 4, 2, 192, 256), BF),
            pltpu.VMEM((4, 576, 256), F32),
            pltpu.VMEM((4, 8, 256), F32),
            pltpu.VMEM((576, 3072), BF),
            pltpu.SemaphoreType.DMA,
            pltpu.SemaphoreType.DMA((4,)),
            pltpu.SemaphoreType.DMA((4, 2, 4)),
            pltpu.SemaphoreType.DMA((4, 2, 4)),
            pltpu.SemaphoreType.DMA((8, 4, 2)),
        ],
        compiler_params=pltpu.CompilerParams(
            collective_id=0, has_side_effects=True, vmem_limit_bytes=56 << 20
        ),
        name="attend_gather_project",
    )(lengths, q, k, v, wt, rate)


def forward(u, w2b, xt, st):
    sq = u * u
    t = jnp.tanh(u * (GC + (GC * GA) * sq))
    half = 0.5 + 0.5 * t
    hb = (u * half).astype(BF)
    z = nn(w2b, hb)
    center = z - jnp.mean(z, axis=0, keepdims=True)
    rs = lax.rsqrt(jnp.mean(center * center, axis=0, keepdims=True) + 1e-5)
    y = center * rs
    return sq, t, half, hb, rs, y, y + (xt - st)


def scan_items(get, put, ready, leave, w10, w2t0, w1s, w2s, w2ts, ub, xs, rprev, count):
    left = lax.broadcasted_iota(jnp.int32, (64, 128), 1) < 64
    left1 = lax.broadcasted_iota(jnp.int32, (1, 128), 1) < 64
    zero = jnp.zeros((64, 128), F32)
    zero1 = jnp.zeros((1, 128), F32)
    w1s[...] = w10.T
    w2s[...] = w2t0
    w2ts[...] = w2t0.T
    ready(0)
    x0 = jnp.where(left, get(0, 64, 64), zero)
    ub[...] = nn(w1s[...].astype(BF), x0.astype(BF))
    xs[...] = x0.T.astype(BF)

    def step(xt, st, eta, xnt):
        xntb = xnt.astype(BF)
        u = ub[...]
        sq, t, half, hb, rs, y, r = forward(u, w2s[...].astype(BF), xt, st)
        dy = r * (eta * (1.0 / 64.0))
        m1 = jnp.mean(dy, axis=0, keepdims=True)
        m2 = jnp.mean(dy * y, axis=0, keepdims=True)
        dzb = (rs * (dy - m1 - y * m2)).astype(BF)
        slope = half + (0.5 * u) * ((1.0 - t * t) * (GC + (3.0 * GC * GA) * sq))
        dub = (nn(w2ts[...].astype(BF), dzb) * slope).astype(BF)
        x = xs[...]
        w1 = w1s[...]
        ub[...] = nn(w1.astype(BF), xntb) - nn(dub, nn(x, xntb).astype(BF))
        w1s[...] = w1 - nn(dub, x)
        w2s[...] -= nt(dzb, hb)
        w2ts[...] -= nt(hb, dzb)
        xs[...] = xnt.T.astype(BF)
        return r

    def segment(s, carry):
        prev = jnp.maximum(s - 1, 0)

        @pl.when(s + 1 < count)
        def _():
            ready(s + 1)

        qs, ks, vs = get(s, 0, 64), get(s, 64, 64), get(s, 128, 64)
        qp = get(prev, 0, 64)
        kn = get(jnp.minimum(s + 1, count - 1), 64, 64)
        rate = get(s, 192, 1)
        mid = jnp.where(left, qs, ks)
        even = step(
            jnp.where(left, ks, qp), jnp.where(left, vs, zero), jnp.where(left1, rate, zero1), mid
        )
        put(prev, jnp.where(left, rprev[...], even).astype(BF))
        rprev[...] = step(
            mid, jnp.where(left, zero, vs), jnp.where(left1, zero1, rate), jnp.where(left, kn, qs)
        )

        @pl.when(s > 0)
        def _():
            leave(prev)

        return carry

    rprev[...] = zero
    lax.fori_loop(0, count, segment, 0)
    last = forward(ub[...], w2s[...].astype(BF), get(count - 1, 0, 64), zero)[-1]
    put(count - 1, jnp.where(left, rprev[...], last).astype(BF))


SCAN_SCRATCH = [
    pltpu.VMEM((256, 64), F32),
    pltpu.VMEM((64, 256), F32),
    pltpu.VMEM((256, 64), F32),
    pltpu.VMEM((256, 128), F32),
    pltpu.VMEM((128, 64), BF),
    pltpu.VMEM((64, 128), F32),
]


def scan_kernel(items, w1, w2t, res, qkv, outs, isem, qsem, osem, rsem, *scratch):
    me = lax.axis_index("seg")
    barrier = pltpu.get_barrier_semaphore()

    def greet(k, carry):
        peer = lax.rem(me + k, 32)
        pl.semaphore_signal(barrier, inc=1, device_id={"seg": peer}, device_id_type=MESH)
        return carry

    lax.fori_loop(1, 32, greet, 0)
    pl.semaphore_wait(barrier, 31)

    def item_out(i):
        return pltpu.make_async_remote_copy(
            src_ref=items.at[i],
            dst_ref=qkv.at[me],
            send_sem=isem.at[i],
            recv_sem=qsem.at[me],
            device_id={"seg": i},
            device_id_type=MESH,
        )

    def item_in(s):
        return pltpu.make_async_remote_copy(
            src_ref=items.at[0],
            dst_ref=qkv.at[s],
            send_sem=isem.at[0],
            recv_sem=qsem.at[s],
            device_id={"seg": s},
            device_id_type=MESH,
        )

    own = jnp.minimum(me, 23)
    video, head = own // 3, lax.rem(own, 3)

    def item_own():
        return pltpu.make_async_copy(items.at[own], qkv.at[own], qsem.at[own])

    def home(s):
        return pltpu.make_async_remote_copy(
            src_ref=outs.at[s],
            dst_ref=res.at[video, pl.ds(pl.multiple_of(64 * head, 64), 64), :],
            send_sem=osem.at[s],
            recv_sem=rsem.at[own],
            device_id={"seg": s},
            device_id_type=MESH,
        )

    def home_own():
        return pltpu.make_async_copy(
            outs.at[own],
            res.at[video, pl.ds(pl.multiple_of(64 * head, 64), 64), :],
            rsem.at[own],
        )

    def home_in(i):
        return pltpu.make_async_remote_copy(
            src_ref=outs.at[0],
            dst_ref=res.at[i // 3, pl.ds(pl.multiple_of(64 * lax.rem(i, 3), 64), 64), :],
            send_sem=osem.at[0],
            recv_sem=rsem.at[i],
            device_id={"seg": i},
            device_id_type=MESH,
        )

    @pl.when(me < 24)
    def _():
        item_own().start()

    def send(k, carry):
        i = lax.rem(me + k, 24)

        @pl.when(i != me)
        def _():
            item_out(i).start()

        return carry

    lax.fori_loop(0, 24, send, 0)

    def leave_home(s):
        @pl.when(s == me)
        def _():
            home_own().start()

        @pl.when(s != me)
        def _():
            home(s).start()

    @pl.when(me < 24)
    def _():
        def get(s, row, rows):
            return qkv[s, row : row + rows, :].astype(F32)

        def put(s, value):
            outs[s] = value

        def ready(s):
            @pl.when(s == me)
            def _():
                item_own().wait()

            @pl.when(s != me)
            def _():
                item_in(s).wait_recv()

        scan_items(get, put, ready, leave_home, w1[head], w2t[head], *scratch, 32)

    def drain_sends(i, carry):
        @pl.when(i != me)
        def _():
            item_out(i).wait_send()

        return carry

    lax.fori_loop(0, 24, drain_sends, 0)

    @pl.when(me < 24)
    def _():
        leave_home(31)

    def drain_items(i, carry):
        @pl.when(i != me)
        def _():
            home_in(i).wait_recv()

        @pl.when(i == me)
        def _():
            home_own().wait()

        return carry

    lax.fori_loop(0, 24, drain_items, 0)

    @pl.when(me < 24)
    def _():
        def drain_homes(s, carry):
            @pl.when(s != me)
            def _():
                home(s).wait_send()

            return carry

        lax.fori_loop(0, 32, drain_homes, 0)


def run_scan(items, w1, w2t):
    return pl.pallas_call(
        scan_kernel,
        out_shape=jax.ShapeDtypeStruct((8, 192, 128), BF),
        in_specs=[VMEM_SPEC] * 3,
        out_specs=VMEM_SPEC,
        scratch_shapes=[
            pltpu.VMEM((32, 208, 128), BF),
            pltpu.VMEM((32, 64, 128), BF),
            pltpu.SemaphoreType.DMA((24,)),
            pltpu.SemaphoreType.DMA((32,)),
            pltpu.SemaphoreType.DMA((32,)),
            pltpu.SemaphoreType.DMA((24,)),
        ]
        + SCAN_SCRATCH,
        compiler_params=pltpu.CompilerParams(collective_id=1, has_side_effects=True),
        name="ttt_scan",
    )(items, w1, w2t)


def body(attn_query, attn_key, attn_value, prompt_len, ttt_weight, init_w1, init_w2t, step_rate):
    def turned(array):
        return jnp.swapaxes(array, 1, 2)

    items = gather_project(
        prompt_len,
        turned(attn_query),
        turned(attn_key),
        turned(attn_value),
        ttt_weight.T,
        jnp.swapaxes(step_rate, 0, 1),
    )
    results = run_scan(items, init_w1, init_w2t)
    return turned(results)


def solution(mesh):
    in_specs = (
        P(None, "seg", "head"),
        P(None, "seg", "head"),
        P(None, "seg", "head"),
        P(None, "seg"),
        P(None, "head"),
        P("head", None, None),
        P("head", None, None),
        P(None, "head", "seg"),
    )
    return jax.shard_map(
        body, mesh=mesh, in_specs=in_specs, out_specs=P(None, "seg", "head"), check_vma=False
    )
```

```python
import math

import jax
import jax.numpy as jnp
from jax import lax
from jax.experimental import pallas as pl
from jax.experimental.pallas import tpu as pltpu
from jax.sharding import PartitionSpec as P

F32, BF = jnp.float32, jnp.bfloat16
GC = math.sqrt(2.0 / math.pi)
GA = 0.044715
MESH = pl.DeviceIdType.MESH
VMEM_SPEC = pl.BlockSpec(memory_space=pltpu.VMEM)


def nn(a, b):
    return lax.dot_general(a, b, (((1,), (0,)), ((), ())), preferred_element_type=F32)


def nt(a, b):
    return lax.dot_general(a, b, (((1,), (1,)), ((), ())), preferred_element_type=F32)


def tn(a, b):
    return lax.dot_general(a, b, (((0,), (0,)), ((), ())), preferred_element_type=F32)


def attend(q, k, v, length, put):
    position = lax.broadcasted_iota(jnp.int32, (128, 1), 0)
    usable = (position >= 64) | (position < length)
    for h in range(3):
        rows = slice(64 * h, 64 * h + 64)
        scores = tn(k[rows, :], q[rows, :]) * 0.125
        scores = jnp.where(usable, scores, -1e30)
        exponent = jnp.exp(scores - jnp.max(scores, axis=0, keepdims=True))
        weights = (exponent * (1.0 / jnp.sum(exponent, axis=0, keepdims=True))).astype(BF)
        put(h, nn(v[rows, :], weights).astype(BF))


def item_of(video, group, head):
    return (video * 2 + group) * 3 + head


def gather_kernel(
    lengths, q, k, v, wt, rate, w1, w2t, out, wsel,
    buf, pbuf, acc, ssq, wv, wb, rate2,
    wsem, isem, psem, rsem, lsem, recv, usem, urecv, dsem, drecv, xrs, xls, msem, wrecv,
):
    me_h, me_s = lax.axis_index("head"), lax.axis_index("seg")
    z, y = me_h // 2, lax.rem(me_h, 2)
    row, x, core = me_s // 8, lax.rem(me_s // 2, 4), lax.rem(me_s, 2)
    other = 1 - y

    def device(seg, head):
        return {"seg": seg, "head": head}

    right, left = device(me_s, lax.rem(me_h + 2, 16)), device(me_s, lax.rem(me_h + 14, 16))
    partner = device(me_s, 2 * z + other)
    above = device(lax.rem(me_s + 8, 32), 2 * z + lax.rem(y + (row + 1) // 4, 2))
    below = device(lax.rem(me_s + 24, 32), 2 * z + lax.rem(y + (4 - row) // 4, 2))
    xup = device(8 * row + 2 * lax.rem(x + 1, 4) + core, me_h)
    xdown = device(8 * row + 2 * lax.rem(x + 3, 4) + core, me_h)
    mate = device(8 * row + 2 * x + 1 - core, me_h)
    barrier = pltpu.get_barrier_semaphore()
    for peer in (right, left, partner, above, below, xup, xdown, mate):
        pl.semaphore_signal(barrier, inc=1, device_id=peer, device_id_type=MESH)
    load = pltpu.make_async_copy(wt, wv, wsem)
    load.start()
    pl.semaphore_wait(barrier, 8)

    def remote(src, dst, send, receive, peer):
        return pltpu.make_async_remote_copy(
            src_ref=src, dst_ref=dst, send_sem=send, recv_sem=receive,
            device_id=peer, device_id_type=MESH,
        )

    item = jnp.minimum(me_s, 23)
    head, group = lax.rem(item, 3), lax.rem(item // 3, 2)

    def start_weight(n):
        source = w1 if n == 0 else w2t
        return remote(source.at[head], wsel.at[n], isem.at[2 + n], isem.at[n], partner)

    def start_local(n):
        source = w1 if n == 0 else w2t
        return pltpu.make_async_copy(source.at[head], wsel.at[n], isem.at[n])

    rates = remote(rate, rate2, isem.at[4], isem.at[5], partner)
    rates.start()

    @pl.when(group == y)
    def _():
        for n in range(2):
            start_local(n).start()
            start_weight(n).start()


    def block(zo, c, yo, sem, peer):
        return remote(buf.at[zo, c, yo], buf.at[zo, c, yo], sem, recv.at[zo, c, yo], peer)

    def to_right(zo, c, yo, d, o):
        return block(zo, c, yo, rsem.at[d, o, c], right)

    def to_left(zo, c, yo, d, o):
        return block(zo, c, yo, lsem.at[d, o, c], left)

    def to_partner(c):
        return remote(pbuf.at[c], buf.at[z, c, y], psem.at[c], recv.at[z, c, y], partner)

    zc = 2 * x + core

    def upper(n):
        return pl.ds(96 * n, 96)

    def lower(n):
        return pl.ds(288 + 96 * n, 96)

    lanes = pl.ds(pl.multiple_of(zc * 384, 128), 384)

    def up_first(n):
        return remote(wv.at[upper(n), lanes], wb.at[zc, upper(n), :], usem.at[n], urecv.at[n], above)

    def up_next(n):
        return remote(wb.at[zc, upper(n), :], wb.at[zc, upper(n), :], usem.at[n], urecv.at[n], above)

    def down_first(n):
        return remote(wv.at[lower(n), lanes], wb.at[zc, lower(n), :], dsem.at[n], drecv.at[n], below)

    def down_next(n):
        return remote(wb.at[zc, lower(n), :], wb.at[zc, lower(n), :], dsem.at[n], drecv.at[n], below)

    def weight(chunk, g, sem, peer):
        part = wb.at[chunk, pl.ds(288 * g, 288), :]
        return remote(part, part, sem, wrecv.at[chunk, g], peer)

    def to_mate(dx, g):
        return weight(2 * lax.rem(x + dx, 4) + core, g, msem.at[dx, g], mate)

    def attend_pair(pair, put_half):
        for half in range(2):
            video = 2 * pair + half

            def put(h, value):
                put_half(slice(64 * h, 64 * h + 64), slice(128 * half, 128 * half + 128), value)

            attend(q[video], k[video], v[video], lengths[video, 0], put)

    def attend_partner(c, carry):
        def put_half(rows, cols, value):
            pbuf[c, rows, cols] = value

        attend_pair(2 * other + c, put_half)

        @pl.when(c == 1)
        def _():
            to_partner(0).start()

        return carry

    lax.fori_loop(0, 2, attend_partner, 0)
    load.wait()

    @pl.when(row == 3)
    def _():
        for n in range(3):
            up_first(n).start()

    @pl.when(row == 0)
    def _():
        for n in range(3):
            down_first(n).start()

    def attend_own(c, carry):
        def put_half(rows, cols, value):
            buf[z, c, y, rows, cols] = value

        attend_pair(2 * y + c, put_half)

        @pl.when(c == 0)
        def _():
            to_partner(1).start()

        @pl.when(c == 1)
        def _():
            to_right(z, 0, y, 0, 0).start()
            to_left(z, 0, y, 0, 0).start()

        return carry

    lax.fori_loop(0, 2, attend_own, 0)

    def relay(n, carry):
        up_next(n).wait_recv()

        @pl.when(row < 3)
        def _():
            up_next(n).start()

        down_next(n).wait_recv()

        @pl.when(row > 0)
        def _():
            down_next(n).start()

        @pl.when(n < 2)
        def _():
            block(z, n, other, psem.at[n], partner).wait_recv()
            to_right(z, n, other, 0, 1).start()
            to_left(z, n, other, 0, 1).start()

        return carry

    acc[...] = jnp.zeros((2, 2, 576, 256), F32)
    ssq[...] = jnp.zeros((2, 8, 256), F32)
    to_right(z, 1, y, 0, 0).start()
    to_left(z, 1, y, 0, 0).start()
    lax.fori_loop(0, 3, relay, 0)
    for g in range(2):
        weight(zc, g, xrs.at[g], xup).start()
        weight(zc, g, xls.at[g], xdown).start()
        to_mate(0, g).start()

    def add(zo, c):
        xb = buf[zo, c].reshape(384, 256)
        w = wv[:, pl.ds(pl.multiple_of(zo * 384, 128), 384)]
        acc[0, c] += nn(w, xb)
        xf = xb.astype(F32)
        ssq[c] += jnp.sum((xf * xf).reshape(48, 8, 256), axis=0)

    def add_other(zo, c):
        acc[1, c] += nn(wb[zo], buf[zo, c].reshape(384, 256))

    def source(j, d):
        return lax.rem(z + 8 + (1 - 2 * (j // 2)) * d, 8)

    def hop(d, carry):
        zr, zl = lax.rem(z + 8 - d, 8), lax.rem(z + d, 8)
        for o in range(2):
            yo = y if o == 0 else other

            def chunk(c, inner):
                to_right(zr, c, yo, 0, 0).wait_recv()

                @pl.when((d < 3) | (c == 0))
                def _():
                    to_right(zr, c, yo, d, o).start()

                to_left(zl, c, yo, 0, 0).wait_recv()

                @pl.when((d < 3) | (c == 1))
                def _():
                    to_left(zl, c, yo, d, o).start()

                return inner

            lax.fori_loop(0, 2, chunk, 0)

        def add_hop(j, inner):
            add(source(j, d - 1), lax.rem(j, 2))
            return inner

        lax.fori_loop(0, jnp.minimum(2 * d, 4), add_hop, 0)

        @pl.when(d == 1)
        def _():
            behind, ahead = 2 * lax.rem(x + 3, 4) + core, 2 * lax.rem(x + 1, 4) + core
            weight(behind, 0, xrs.at[0], xup).wait_recv()
            weight(behind, 0, xrs.at[2], xup).start()
            weight(ahead, 1, xls.at[1], xdown).wait_recv()
            weight(ahead, 1, xls.at[2], xdown).start()
            to_mate(3, 0).start()
            to_mate(1, 1).start()
            weight(behind, 1, xrs.at[1], xup).wait_recv()
            to_mate(3, 1).start()
            weight(ahead, 0, xls.at[0], xdown).wait_recv()
            to_mate(1, 0).start()

        @pl.when(d == 2)
        def _():
            far = 2 * lax.rem(x + 2, 4) + core
            for g in range(2):
                weight(far, g, xrs.at[2], xup).wait_recv()
                to_mate(2, g).start()

        return carry

    lax.fori_loop(1, 4, hop, 0)

    def from_mate(n, carry):
        for g in range(2):
            weight(2 * n + 1 - core, g, msem.at[0, 0], mate).wait_recv()
        return carry

    lax.fori_loop(0, 4, from_mate, 0)

    def add_last(j, inner):
        add(source(j, 3), lax.rem(j, 2))
        return inner

    lax.fori_loop(0, 4, add_last, 0)

    def other_group(n, carry):
        add_other(lax.rem(z + 5 + n // 2, 8), lax.rem(n, 2))
        return carry

    lax.fori_loop(0, 14, other_group, 0)
    opposite = lax.rem(z + 4, 8)

    def final(c, carry):
        for o in range(2):
            yo = y if o == 0 else other

            @pl.when(c == 0)
            def _():
                to_right(opposite, c, yo, 0, 0).wait_recv()

            @pl.when(c == 1)
            def _():
                to_left(opposite, c, yo, 0, 0).wait_recv()

        add(opposite, c)
        add_other(opposite, c)
        return carry

    lax.fori_loop(0, 2, final, 0)
    rates.wait_recv()
    position = lax.broadcasted_iota(jnp.int32, (1, 128), 1)

    def finish(c, carry):
        mean = jnp.sum(ssq[c], axis=0, keepdims=True) * (1.0 / 3072.0)
        scale = lax.rsqrt(mean + 1e-6)
        for g in range(2):
            projected = (acc[g, c] * scale).astype(BF)
            source_rate = rate if g == 0 else rate2
            for half in range(2):
                video = 4 * y + 2 * c + half
                usable = (position >= 64) | (position < lengths[video, 0])
                for h in range(3):
                    slot = item_of(2 * c + half, y if g == 0 else other, h)
                    out[slot, 0:192, :] = projected[
                        192 * h : 192 * h + 192, 128 * half : 128 * half + 128
                    ]
                    eta = jnp.where(usable, source_rate[h, pl.ds(video, 1), :], 0.0)
                    out[slot, 192:208, :] = jnp.broadcast_to(eta, (16, 128)).astype(BF)
        return carry

    lax.fori_loop(0, 2, finish, 0)


    rates.wait_send()

    @pl.when(group == y)
    def _():
        for n in range(2):
            start_local(n).wait()
            start_weight(n).wait_send()

    @pl.when(group != y)
    def _():
        for n in range(2):
            start_weight(n).wait_recv()

    @pl.when(row < 3)
    def _():
        for n in range(3):
            up_next(n).wait_send()

    @pl.when(row == 3)
    def _():
        for n in range(3):
            up_first(n).wait_send()

    @pl.when(row > 0)
    def _():
        for n in range(3):
            down_next(n).wait_send()

    @pl.when(row == 0)
    def _():
        for n in range(3):
            down_first(n).wait_send()

    for n in range(3):
        weight(zc, 0, xrs.at[n], xup).wait_send()
        weight(zc, 0, xls.at[n], xdown).wait_send()
    for dx in range(4):
        for g in range(2):
            to_mate(dx, g).wait_send()

    def drain(c, carry):
        to_partner(c).wait_send()
        for o in range(2):
            for d in range(3):
                to_right(z, c, y, d, o).wait_send()
                to_left(z, c, y, d, o).wait_send()

            @pl.when(c == 0)
            def _():
                to_right(z, c, y, 3, o).wait_send()

            @pl.when(c == 1)
            def _():
                to_left(z, c, y, 3, o).wait_send()

        return carry

    lax.fori_loop(0, 2, drain, 0)


def gather_project(lengths, q, k, v, wt, rate, w1, w2t):
    any_spec = pl.BlockSpec(memory_space=pl.ANY)
    dma = pltpu.SemaphoreType.DMA
    return pl.pallas_call(
        gather_kernel,
        out_shape=(
            jax.ShapeDtypeStruct((24, 208, 128), BF),
            jax.ShapeDtypeStruct((2, 64, 256), F32),
        ),
        in_specs=[
            pl.BlockSpec(memory_space=pltpu.SMEM),
            VMEM_SPEC,
            VMEM_SPEC,
            VMEM_SPEC,
            any_spec,
            VMEM_SPEC,
            VMEM_SPEC,
            VMEM_SPEC,
        ],
        out_specs=(VMEM_SPEC, VMEM_SPEC),
        scratch_shapes=[
            pltpu.VMEM((8, 2, 2, 192, 256), BF),
            pltpu.VMEM((2, 192, 256), BF),
            pltpu.VMEM((2, 2, 576, 256), F32),
            pltpu.VMEM((2, 8, 256), F32),
            pltpu.VMEM((576, 3072), BF),
            pltpu.VMEM((8, 576, 384), BF),
            pltpu.VMEM((3, 8, 128), F32),
            dma,
            dma((6,)),
            dma((2,)),
            dma((4, 2, 2)),
            dma((4, 2, 2)),
            dma((8, 2, 2)),
            dma((3,)),
            dma((3,)),
            dma((3,)),
            dma((3,)),
            dma((3,)),
            dma((3,)),
            dma((4, 2)),
            dma((8, 2)),
        ],
        compiler_params=pltpu.CompilerParams(
            collective_id=0, has_side_effects=True, vmem_limit_bytes=56 << 20
        ),
        name="attend_gather_project",
    )(lengths, q, k, v, wt, rate, w1, w2t)


def forward(u, w2b, xt, st):
    sq = u * u
    t = jnp.tanh(u * (GC + (GC * GA) * sq))
    half = 0.5 + 0.5 * t
    hb = (u * half).astype(BF)
    z = nn(w2b, hb)
    center = z - jnp.mean(z, axis=0, keepdims=True)
    rs = lax.rsqrt(jnp.mean(center * center, axis=0, keepdims=True) + 1e-5)
    y = center * rs
    return sq, t, half, hb, rs, y, y + (xt - st)


def scan_items(get, put, ready, leave, w10, w2t0, w1s, w2s, w2ts, ub, xs, rprev, count):
    left = lax.broadcasted_iota(jnp.int32, (64, 128), 1) < 64
    left1 = lax.broadcasted_iota(jnp.int32, (1, 128), 1) < 64
    zero = jnp.zeros((64, 128), F32)
    zero1 = jnp.zeros((1, 128), F32)
    w1s[...] = w10.T
    w2s[...] = w2t0
    w2ts[...] = w2t0.T
    ready(0)
    x0 = jnp.where(left, get(0, 64, 64), zero)
    ub[...] = nn(w1s[...].astype(BF), x0.astype(BF))
    xs[...] = x0.T.astype(BF)

    def step(xt, st, eta, xnt):
        xntb = xnt.astype(BF)
        u = ub[...]
        sq, t, half, hb, rs, y, r = forward(u, w2s[...].astype(BF), xt, st)
        dy = r * (eta * (1.0 / 64.0))
        m1 = jnp.mean(dy, axis=0, keepdims=True)
        m2 = jnp.mean(dy * y, axis=0, keepdims=True)
        dzb = (rs * (dy - m1 - y * m2)).astype(BF)
        slope = half + (0.5 * u) * ((1.0 - t * t) * (GC + (3.0 * GC * GA) * sq))
        dub = (nn(w2ts[...].astype(BF), dzb) * slope).astype(BF)
        x = xs[...]
        w1 = w1s[...]
        ub[...] = nn(w1.astype(BF), xntb) - nn(dub, nn(x, xntb).astype(BF))
        w1s[...] = w1 - nn(dub, x)
        w2s[...] -= nt(dzb, hb)
        w2ts[...] -= nt(hb, dzb)
        xs[...] = xnt.T.astype(BF)
        return r

    def segment(s, carry):
        prev = jnp.maximum(s - 1, 0)

        @pl.when(s + 1 < count)
        def _():
            ready(s + 1)

        qs, ks, vs = get(s, 0, 64), get(s, 64, 64), get(s, 128, 64)
        qp = get(prev, 0, 64)
        kn = get(jnp.minimum(s + 1, count - 1), 64, 64)
        rate = get(s, 192, 1)
        mid = jnp.where(left, qs, ks)
        even = step(
            jnp.where(left, ks, qp), jnp.where(left, vs, zero), jnp.where(left1, rate, zero1), mid
        )
        put(prev, jnp.where(left, rprev[...], even).astype(BF))
        rprev[...] = step(
            mid, jnp.where(left, zero, vs), jnp.where(left1, zero1, rate), jnp.where(left, kn, qs)
        )

        @pl.when(s > 0)
        def _():
            leave(prev)

        return carry

    rprev[...] = zero
    lax.fori_loop(0, count, segment, 0)
    last = forward(ub[...], w2s[...].astype(BF), get(count - 1, 0, 64), zero)[-1]
    put(count - 1, jnp.where(left, rprev[...], last).astype(BF))


SCAN_SCRATCH = [
    pltpu.VMEM((256, 64), F32),
    pltpu.VMEM((64, 256), F32),
    pltpu.VMEM((256, 64), F32),
    pltpu.VMEM((256, 128), F32),
    pltpu.VMEM((128, 64), BF),
    pltpu.VMEM((64, 128), F32),
]


def scan_kernel(items, wsel, res, qkv, outs, isem, qsem, osem, rsem, *scratch):
    me, me_h = lax.axis_index("seg"), lax.axis_index("head")
    z, y = me_h // 2, lax.rem(me_h, 2)
    barrier = pltpu.get_barrier_semaphore()

    def greet(k, carry):
        peer = lax.rem(me + k, 32)
        pl.semaphore_signal(
            barrier, inc=1, device_id={"seg": peer, "head": me_h}, device_id_type=MESH
        )
        pl.semaphore_signal(
            barrier, inc=1, device_id={"seg": peer, "head": 2 * z + 1 - y}, device_id_type=MESH
        )
        return carry

    lax.fori_loop(1, 32, greet, 0)
    pl.semaphore_signal(
        barrier, inc=1, device_id={"seg": me, "head": 2 * z + 1 - y}, device_id_type=MESH
    )
    pl.semaphore_wait(barrier, 63)

    def item_out(i):
        return pltpu.make_async_remote_copy(
            src_ref=items.at[i],
            dst_ref=qkv.at[me],
            send_sem=isem.at[i],
            recv_sem=qsem.at[me],
            device_id={"seg": i, "head": me_h},
            device_id_type=MESH,
        )

    def item_in(s):
        return pltpu.make_async_remote_copy(
            src_ref=items.at[0],
            dst_ref=qkv.at[s],
            send_sem=isem.at[0],
            recv_sem=qsem.at[s],
            device_id={"seg": s, "head": me_h},
            device_id_type=MESH,
        )

    own = jnp.minimum(me, 23)
    video, group, head = 4 * y + own // 6, lax.rem(own // 3, 2), lax.rem(own, 3)

    def place(v, h):
        return res.at[v, pl.ds(pl.multiple_of(64 * h, 64), 64), :]

    def item_own():
        return pltpu.make_async_copy(items.at[own], qkv.at[own], qsem.at[own])

    def home(s):
        return pltpu.make_async_remote_copy(
            src_ref=outs.at[s],
            dst_ref=place(video, head),
            send_sem=osem.at[s],
            recv_sem=rsem.at[video * 3 + head],
            device_id={"seg": s, "head": 2 * z + group},
            device_id_type=MESH,
        )

    def home_own():
        return pltpu.make_async_copy(outs.at[own], place(video, head), rsem.at[video * 3 + head])

    def home_in(n):
        return pltpu.make_async_remote_copy(
            src_ref=outs.at[0],
            dst_ref=place(n // 3, lax.rem(n, 3)),
            send_sem=osem.at[0],
            recv_sem=rsem.at[n],
            device_id={"seg": me, "head": 2 * z + 1 - y},
            device_id_type=MESH,
        )

    def stays(s):
        return (s == me) & (group == y)

    @pl.when(me < 24)
    def _():
        item_own().start()

    def send(k, carry):
        i = lax.rem(me + k, 24)

        @pl.when(i != me)
        def _():
            item_out(i).start()

        return carry

    lax.fori_loop(0, 24, send, 0)

    def leave_home(s):
        @pl.when(stays(s))
        def _():
            home_own().start()

        @pl.when(jnp.logical_not(stays(s)))
        def _():
            home(s).start()

    @pl.when(me < 24)
    def _():
        def get(s, row, rows):
            return qkv[s, row : row + rows, :].astype(F32)

        def put(s, value):
            outs[s] = value

        def ready(s):
            @pl.when(s == me)
            def _():
                item_own().wait()

            @pl.when(s != me)
            def _():
                item_in(s).wait_recv()

        scan_items(get, put, ready, leave_home, wsel[0], wsel[1], *scratch, 32)

    def drain_sends(i, carry):
        @pl.when(i != me)
        def _():
            item_out(i).wait_send()

        return carry

    lax.fori_loop(0, 24, drain_sends, 0)

    @pl.when(me < 24)
    def _():
        leave_home(31)

    mine = (me < 24) & (group == y)

    def drain_items(n, carry):
        local = mine & (n == video * 3 + head)

        @pl.when(local)
        def _():
            home_own().wait()

        @pl.when(jnp.logical_not(local))
        def _():
            home_in(n).wait_recv()

        return carry

    lax.fori_loop(0, 24, drain_items, 0)

    @pl.when(me < 24)
    def _():
        def drain_homes(s, carry):
            @pl.when(jnp.logical_not(stays(s)))
            def _():
                home(s).wait_send()

            return carry

        lax.fori_loop(0, 32, drain_homes, 0)


def run_scan(items, wsel):
    return pl.pallas_call(
        scan_kernel,
        out_shape=jax.ShapeDtypeStruct((8, 192, 128), BF),
        in_specs=[VMEM_SPEC] * 2,
        out_specs=VMEM_SPEC,
        scratch_shapes=[
            pltpu.VMEM((32, 208, 128), BF),
            pltpu.VMEM((32, 64, 128), BF),
            pltpu.SemaphoreType.DMA((24,)),
            pltpu.SemaphoreType.DMA((32,)),
            pltpu.SemaphoreType.DMA((32,)),
            pltpu.SemaphoreType.DMA((24,)),
        ]
        + SCAN_SCRATCH,
        compiler_params=pltpu.CompilerParams(collective_id=1, has_side_effects=True),
        name="ttt_scan",
    )(items, wsel)


def body(attn_query, attn_key, attn_value, prompt_len, ttt_weight, init_w1, init_w2t, step_rate):
    def turned(array):
        return jnp.swapaxes(array, 1, 2)

    items, wsel = gather_project(
        prompt_len,
        turned(attn_query),
        turned(attn_key),
        turned(attn_value),
        ttt_weight.T,
        jnp.swapaxes(step_rate, 0, 1),
        init_w1,
        init_w2t,
    )
    results = run_scan(items, wsel)
    return turned(results)


def solution(mesh):
    in_specs = (
        P(None, "seg", "head"),
        P(None, "seg", "head"),
        P(None, "seg", "head"),
        P(None, "seg"),
        P(None, "head"),
        P("head", None, None),
        P("head", None, None),
        P(None, "head", "seg"),
    )
    return jax.shard_map(
        body, mesh=mesh, in_specs=in_specs, out_specs=P(None, "seg", "head"), check_vma=False
    )
```

```python
import math

import jax
import jax.numpy as jnp
from jax import lax
from jax.experimental import pallas as pl
from jax.experimental.pallas import tpu as pltpu
from jax.sharding import PartitionSpec as P

F32, BF = jnp.float32, jnp.bfloat16
GC = math.sqrt(2.0 / math.pi)
GA = 0.044715
MESH = pl.DeviceIdType.MESH
VMEM_SPEC = pl.BlockSpec(memory_space=pltpu.VMEM)


def nn(a, b):
    return lax.dot_general(a, b, (((1,), (0,)), ((), ())), preferred_element_type=F32)


def nt(a, b):
    return lax.dot_general(a, b, (((1,), (1,)), ((), ())), preferred_element_type=F32)


def tn(a, b):
    return lax.dot_general(a, b, (((0,), (0,)), ((), ())), preferred_element_type=F32)


def attend(q, k, v, length, put):
    position = lax.broadcasted_iota(jnp.int32, (128, 1), 0)
    usable = (position >= 64) | (position < length)
    for h in range(3):
        rows = slice(64 * h, 64 * h + 64)
        scores = tn(k[rows, :], q[rows, :]) * 0.125
        scores = jnp.where(usable, scores, -1e30)
        exponent = jnp.exp(scores - jnp.max(scores, axis=0, keepdims=True))
        weights = (exponent * (1.0 / jnp.sum(exponent, axis=0, keepdims=True))).astype(BF)
        put(h, nn(v[rows, :], weights).astype(BF))


def item_of(video, group, head):
    return (video * 2 + group) * 3 + head


def gather_kernel(
    lengths, q, k, v, wt, rate, w1, w2t, out, wsel,
    buf, pbuf, acc, ssq, wv, wb, rate2,
    wsem, isem, psem, rsem, lsem, recv, csem, ysend, yrecv, xsem, msem, wrecv,
):
    me_h, me_s = lax.axis_index("head"), lax.axis_index("seg")
    z, y = me_h // 2, lax.rem(me_h, 2)
    row, x, core = me_s // 8, lax.rem(me_s // 2, 4), lax.rem(me_s, 2)
    other = 1 - y

    def device(seg, head):
        return {"seg": seg, "head": head}

    right, left = device(me_s, lax.rem(me_h + 2, 16)), device(me_s, lax.rem(me_h + 14, 16))
    partner = device(me_s, 2 * z + other)
    above = device(lax.rem(me_s + 8, 32), 2 * z + lax.rem(y + (row + 1) // 4, 2))
    below = device(lax.rem(me_s + 24, 32), 2 * z + lax.rem(y + (4 - row) // 4, 2))
    xpeer = [device(8 * row + 2 * lax.rem(x + dx, 4) + core, me_h) for dx in (1, 2, 3)]
    mate = device(8 * row + 2 * x + 1 - core, me_h)
    barrier = pltpu.get_barrier_semaphore()
    for peer in (right, left, partner, above, below, mate, *xpeer):
        pl.semaphore_signal(barrier, inc=1, device_id=peer, device_id_type=MESH)
    load = pltpu.make_async_copy(wt, wv, wsem)
    load.start()
    pl.semaphore_wait(barrier, 9)

    def remote(src, dst, send, receive, peer):
        return pltpu.make_async_remote_copy(
            src_ref=src, dst_ref=dst, send_sem=send, recv_sem=receive,
            device_id=peer, device_id_type=MESH,
        )

    item = jnp.minimum(me_s, 23)
    head, group = lax.rem(item, 3), lax.rem(item // 3, 2)

    def start_weight(n):
        source = w1 if n == 0 else w2t
        return remote(source.at[head], wsel.at[n], isem.at[2 + n], isem.at[n], partner)

    def start_local(n):
        source = w1 if n == 0 else w2t
        return pltpu.make_async_copy(source.at[head], wsel.at[n], isem.at[n])

    rates = remote(rate, rate2, isem.at[4], isem.at[5], partner)
    rates.start()

    @pl.when(group == y)
    def _():
        for n in range(2):
            start_local(n).start()
            start_weight(n).start()


    def block(zo, c, yo, sem, peer):
        return remote(buf.at[zo, c, yo], buf.at[zo, c, yo], sem, recv.at[zo, c, yo], peer)

    def to_right(zo, c, yo, d, o):
        return block(zo, c, yo, rsem.at[d, o, c], right)

    def to_left(zo, c, yo, d, o):
        return block(zo, c, yo, lsem.at[d, o, c], left)

    def to_partner(c):
        return remote(pbuf.at[c], buf.at[z, c, y], psem.at[c], recv.at[z, c, y], partner)

    zc = 2 * x + core
    lanes = pl.ds(pl.multiple_of(zc * 384, 128), 384)

    def half_of(chunk, g):
        return wb.at[chunk, pl.ds(pl.multiple_of(288 * g, 32), 288), :]

    def cross(g, peer):
        source = wv.at[pl.ds(288 * g, 288), lanes]
        return remote(source, half_of(zc, g), csem, yrecv.at[g], peer)

    def onward(g):
        peer = device(lax.rem(me_s + 8 + 16 * g, 32), me_h)
        return remote(half_of(zc, g), half_of(zc, g), ysend.at[g], yrecv.at[g], peer)

    def weight(chunk, g, sem, peer):
        return remote(half_of(chunk, g), half_of(chunk, g), sem, wrecv.at[chunk, g], peer)

    def chunk_at(dx):
        return 2 * lax.rem(x + dx, 4) + core

    def to_mate(dx, g):
        return weight(chunk_at(dx), g, msem.at[dx, g], mate)

    def spread(g):
        for dx in (1, 3, 2):
            weight(zc, g, xsem.at[dx - 1, g], xpeer[dx - 1]).start()
        to_mate(0, g).start()

    sooner = row // 2
    later = 1 - sooner
    edge = (row == 0) | (row == 3)

    def attend_pair(pair, put_half):
        for half in range(2):
            video = 2 * pair + half

            def put(h, value):
                put_half(slice(64 * h, 64 * h + 64), slice(128 * half, 128 * half + 128), value)

            attend(q[video], k[video], v[video], lengths[video, 0], put)

    def hop(d, o):
        yo = y if o == 0 else other
        zr, zl = lax.rem(z + 8 - d, 8), lax.rem(z + d, 8)
        for c in range(2):
            if d < 4 or c == 0:
                to_right(zr, c, yo, 0, 0).wait_recv()
            if d < 3 or (d == 3 and c == 0):
                to_right(zr, c, yo, d, o).start()
            if d < 4 or c == 1:
                to_left(zl, c, yo, 0, 0).wait_recv()
            if d < 3 or (d == 3 and c == 1):
                to_left(zl, c, yo, d, o).start()

    def attend_own(c, carry):
        def put_half(rows, cols, value):
            buf[z, c, y, rows, cols] = value

        attend_pair(2 * y + c, put_half)

        @pl.when(c == 0)
        def _():
            load.wait()

            @pl.when(row == 3)
            def _():
                cross(0, above).start()

            @pl.when(row == 0)
            def _():
                cross(1, below).start()

        @pl.when(c == 1)
        def _():
            to_right(z, 0, y, 0, 0).start()
            to_left(z, 0, y, 0, 0).start()

        return carry

    lax.fori_loop(0, 2, attend_own, 0)

    def attend_partner(c, carry):
        def put_half(rows, cols, value):
            pbuf[c, rows, cols] = value

        attend_pair(2 * other + c, put_half)

        @pl.when(c == 0)
        def _():
            to_right(z, 1, y, 0, 0).start()
            to_left(z, 1, y, 0, 0).start()

        @pl.when(c == 1)
        def _():
            to_partner(0).start()

        return carry

    lax.fori_loop(0, 2, attend_partner, 0)
    acc[...] = jnp.zeros((2, 2, 576, 256), F32)
    ssq[...] = jnp.zeros((2, 8, 256), F32)
    to_partner(1).start()

    @pl.when(edge)
    def _():
        onward(sooner).wait_recv()
        onward(sooner).start()
        spread(sooner)

    hop(1, 0)

    @pl.when(jnp.logical_not(edge))
    def _():
        onward(sooner).wait_recv()
        onward(sooner).start()
        spread(sooner)

    for c in range(2):
        block(z, c, other, psem.at[c], partner).wait_recv()
        to_right(z, c, other, 0, 1).start()
        to_left(z, c, other, 0, 1).start()
    hop(2, 0)

    @pl.when(jnp.logical_not(edge))
    def _():
        onward(later).wait_recv()
        onward(later).start()
        spread(later)

    hop(1, 1)
    hop(3, 0)

    @pl.when(edge)
    def _():
        onward(later).wait_recv()
        spread(later)

    hop(2, 1)
    for dx in (1, 3, 2):
        weight(chunk_at(dx), sooner, csem, mate).wait_recv()
        to_mate(dx, sooner).start()
    hop(3, 1)

    def add(n, carry):
        zo, c = lax.rem(z + 5 + n // 2, 8), lax.rem(n, 2)
        xb = buf[zo, c].reshape(384, 256)
        w = wv[:, pl.ds(pl.multiple_of(zo * 384, 128), 384)]
        acc[0, c] += nn(w, xb)
        xf = xb.astype(F32)
        ssq[c] += jnp.sum((xf * xf).reshape(48, 8, 256), axis=0)
        return carry

    lax.fori_loop(0, 14, add, 0)
    hop(4, 0)
    hop(4, 1)
    lax.fori_loop(14, 16, add, 0)
    for dx in (1, 3, 2):
        weight(chunk_at(dx), later, csem, mate).wait_recv()
        to_mate(dx, later).start()

    def add_other(n, carry):
        zo, c = 2 * lax.rem(n // 2, 4) + lax.rem(core + n // 8, 2), lax.rem(n, 2)

        @pl.when((n >= 8) & (c == 0))
        def _():
            for g in range(2):
                weight(zo, g, csem, mate).wait_recv()

        acc[1, c] += nn(wb[zo], buf[zo, c].reshape(384, 256))
        return carry

    lax.fori_loop(0, 16, add_other, 0)
    rates.wait_recv()
    position = lax.broadcasted_iota(jnp.int32, (1, 128), 1)

    def finish(c, carry):
        mean = jnp.sum(ssq[c], axis=0, keepdims=True) * (1.0 / 3072.0)
        scale = lax.rsqrt(mean + 1e-6)
        for g in range(2):
            projected = (acc[g, c] * scale).astype(BF)
            source_rate = rate if g == 0 else rate2
            for half in range(2):
                video = 4 * y + 2 * c + half
                usable = (position >= 64) | (position < lengths[video, 0])
                for h in range(3):
                    slot = item_of(2 * c + half, y if g == 0 else other, h)
                    out[slot, 0:192, :] = projected[
                        192 * h : 192 * h + 192, 128 * half : 128 * half + 128
                    ]
                    eta = jnp.where(usable, source_rate[h, pl.ds(video, 1), :], 0.0)
                    out[slot, 192:208, :] = jnp.broadcast_to(eta, (16, 128)).astype(BF)
        return carry

    lax.fori_loop(0, 2, finish, 0)


    rates.wait_send()

    @pl.when(group == y)
    def _():
        for n in range(2):
            start_local(n).wait()
            start_weight(n).wait_send()

    @pl.when(group != y)
    def _():
        for n in range(2):
            start_weight(n).wait_recv()

    @pl.when(edge)
    def _():
        cross(0, above).wait_send()

    onward(sooner).wait_send()

    @pl.when(jnp.logical_not(edge))
    def _():
        onward(later).wait_send()

    for g in range(2):
        for dx in range(4):
            to_mate(dx, g).wait_send()
        for dx in range(3):
            weight(zc, g, xsem.at[dx, g], xpeer[dx]).wait_send()

    def drain(c, carry):
        to_partner(c).wait_send()
        for o in range(2):
            for d in range(3):
                to_right(z, c, y, d, o).wait_send()
                to_left(z, c, y, d, o).wait_send()

            @pl.when(c == 0)
            def _():
                to_right(z, c, y, 3, o).wait_send()

            @pl.when(c == 1)
            def _():
                to_left(z, c, y, 3, o).wait_send()

        return carry

    lax.fori_loop(0, 2, drain, 0)


def gather_project(lengths, q, k, v, wt, rate, w1, w2t):
    any_spec = pl.BlockSpec(memory_space=pl.ANY)
    dma = pltpu.SemaphoreType.DMA
    return pl.pallas_call(
        gather_kernel,
        out_shape=(
            jax.ShapeDtypeStruct((24, 208, 128), BF),
            jax.ShapeDtypeStruct((2, 64, 256), F32),
        ),
        in_specs=[
            pl.BlockSpec(memory_space=pltpu.SMEM),
            VMEM_SPEC,
            VMEM_SPEC,
            VMEM_SPEC,
            any_spec,
            VMEM_SPEC,
            VMEM_SPEC,
            VMEM_SPEC,
        ],
        out_specs=(VMEM_SPEC, VMEM_SPEC),
        scratch_shapes=[
            pltpu.VMEM((8, 2, 2, 192, 256), BF),
            pltpu.VMEM((2, 192, 256), BF),
            pltpu.VMEM((2, 2, 576, 256), F32),
            pltpu.VMEM((2, 8, 256), F32),
            pltpu.VMEM((576, 3072), BF),
            pltpu.VMEM((8, 576, 384), BF),
            pltpu.VMEM((3, 8, 128), F32),
            dma,
            dma((6,)),
            dma((2,)),
            dma((4, 2, 2)),
            dma((4, 2, 2)),
            dma((8, 2, 2)),
            dma,
            dma((2,)),
            dma((2,)),
            dma((3, 2)),
            dma((4, 2)),
            dma((8, 2)),
        ],
        compiler_params=pltpu.CompilerParams(
            collective_id=0, has_side_effects=True, vmem_limit_bytes=56 << 20
        ),
        name="attend_gather_project",
    )(lengths, q, k, v, wt, rate, w1, w2t)


def forward(u, w2b, xt, st):
    sq = u * u
    t = jnp.tanh(u * (GC + (GC * GA) * sq))
    half = 0.5 + 0.5 * t
    hb = (u * half).astype(BF)
    z = nn(w2b, hb)
    center = z - jnp.mean(z, axis=0, keepdims=True)
    rs = lax.rsqrt(jnp.mean(center * center, axis=0, keepdims=True) + 1e-5)
    y = center * rs
    return sq, t, half, hb, rs, y, y + (xt - st)


def scan_items(get, put, ready, leave, w10, w2t0, w1s, w2s, w2ts, ub, xs, rprev, count):
    left = lax.broadcasted_iota(jnp.int32, (64, 128), 1) < 64
    left1 = lax.broadcasted_iota(jnp.int32, (1, 128), 1) < 64
    zero = jnp.zeros((64, 128), F32)
    zero1 = jnp.zeros((1, 128), F32)
    w1s[...] = w10.T
    w2s[...] = w2t0
    w2ts[...] = w2t0.T
    ready(0)
    x0 = jnp.where(left, get(0, 64, 64), zero)
    ub[...] = nn(w1s[...].astype(BF), x0.astype(BF))
    xs[...] = x0.T.astype(BF)

    def step(xt, st, eta, xnt):
        xntb = xnt.astype(BF)
        u = ub[...]
        sq, t, half, hb, rs, y, r = forward(u, w2s[...].astype(BF), xt, st)
        dy = r * (eta * (1.0 / 64.0))
        m1 = jnp.mean(dy, axis=0, keepdims=True)
        m2 = jnp.mean(dy * y, axis=0, keepdims=True)
        dzb = (rs * (dy - m1 - y * m2)).astype(BF)
        slope = half + (0.5 * u) * ((1.0 - t * t) * (GC + (3.0 * GC * GA) * sq))
        dub = (nn(w2ts[...].astype(BF), dzb) * slope).astype(BF)
        x = xs[...]
        w1 = w1s[...]
        ub[...] = nn(w1.astype(BF), xntb) - nn(dub, nn(x, xntb).astype(BF))
        w1s[...] = w1 - nn(dub, x)
        w2s[...] -= nt(dzb, hb)
        w2ts[...] -= nt(hb, dzb)
        xs[...] = xnt.T.astype(BF)
        return r

    def segment(s, carry):
        prev = jnp.maximum(s - 1, 0)

        @pl.when(s + 1 < count)
        def _():
            ready(s + 1)

        qs, ks, vs = get(s, 0, 64), get(s, 64, 64), get(s, 128, 64)
        qp = get(prev, 0, 64)
        kn = get(jnp.minimum(s + 1, count - 1), 64, 64)
        rate = get(s, 192, 1)
        mid = jnp.where(left, qs, ks)
        even = step(
            jnp.where(left, ks, qp), jnp.where(left, vs, zero), jnp.where(left1, rate, zero1), mid
        )
        put(prev, jnp.where(left, rprev[...], even).astype(BF))
        rprev[...] = step(
            mid, jnp.where(left, zero, vs), jnp.where(left1, zero1, rate), jnp.where(left, kn, qs)
        )

        @pl.when(s > 0)
        def _():
            leave(prev)

        return carry

    rprev[...] = zero
    lax.fori_loop(0, count, segment, 0)
    last = forward(ub[...], w2s[...].astype(BF), get(count - 1, 0, 64), zero)[-1]
    put(count - 1, jnp.where(left, rprev[...], last).astype(BF))


SCAN_SCRATCH = [
    pltpu.VMEM((256, 64), F32),
    pltpu.VMEM((64, 256), F32),
    pltpu.VMEM((256, 64), F32),
    pltpu.VMEM((256, 128), F32),
    pltpu.VMEM((128, 64), BF),
    pltpu.VMEM((64, 128), F32),
]


def scan_kernel(items, wsel, res, qkv, outs, isem, qsem, osem, rsem, *scratch):
    me, me_h = lax.axis_index("seg"), lax.axis_index("head")
    z, y = me_h // 2, lax.rem(me_h, 2)
    barrier = pltpu.get_barrier_semaphore()

    def greet(k, carry):
        peer = lax.rem(me + k, 32)
        pl.semaphore_signal(
            barrier, inc=1, device_id={"seg": peer, "head": me_h}, device_id_type=MESH
        )
        pl.semaphore_signal(
            barrier, inc=1, device_id={"seg": peer, "head": 2 * z + 1 - y}, device_id_type=MESH
        )
        return carry

    lax.fori_loop(1, 32, greet, 0)
    pl.semaphore_signal(
        barrier, inc=1, device_id={"seg": me, "head": 2 * z + 1 - y}, device_id_type=MESH
    )
    pl.semaphore_wait(barrier, 63)

    def item_out(i):
        return pltpu.make_async_remote_copy(
            src_ref=items.at[i],
            dst_ref=qkv.at[me],
            send_sem=isem.at[i],
            recv_sem=qsem.at[me],
            device_id={"seg": i, "head": me_h},
            device_id_type=MESH,
        )

    def item_in(s):
        return pltpu.make_async_remote_copy(
            src_ref=items.at[0],
            dst_ref=qkv.at[s],
            send_sem=isem.at[0],
            recv_sem=qsem.at[s],
            device_id={"seg": s, "head": me_h},
            device_id_type=MESH,
        )

    own = jnp.minimum(me, 23)
    video, group, head = 4 * y + own // 6, lax.rem(own // 3, 2), lax.rem(own, 3)

    def place(v, h):
        return res.at[v, pl.ds(pl.multiple_of(64 * h, 64), 64), :]

    def item_own():
        return pltpu.make_async_copy(items.at[own], qkv.at[own], qsem.at[own])

    def home(s):
        return pltpu.make_async_remote_copy(
            src_ref=outs.at[s],
            dst_ref=place(video, head),
            send_sem=osem.at[s],
            recv_sem=rsem.at[video * 3 + head],
            device_id={"seg": s, "head": 2 * z + group},
            device_id_type=MESH,
        )

    def home_own():
        return pltpu.make_async_copy(outs.at[own], place(video, head), rsem.at[video * 3 + head])

    def home_in(n):
        return pltpu.make_async_remote_copy(
            src_ref=outs.at[0],
            dst_ref=place(n // 3, lax.rem(n, 3)),
            send_sem=osem.at[0],
            recv_sem=rsem.at[n],
            device_id={"seg": me, "head": 2 * z + 1 - y},
            device_id_type=MESH,
        )

    def stays(s):
        return (s == me) & (group == y)

    @pl.when(me < 24)
    def _():
        item_own().start()

    def send(k, carry):
        i = lax.rem(me + k, 24)

        @pl.when(i != me)
        def _():
            item_out(i).start()

        return carry

    lax.fori_loop(0, 24, send, 0)

    def leave_home(s):
        @pl.when(stays(s))
        def _():
            home_own().start()

        @pl.when(jnp.logical_not(stays(s)))
        def _():
            home(s).start()

    @pl.when(me < 24)
    def _():
        def get(s, row, rows):
            return qkv[s, row : row + rows, :].astype(F32)

        def put(s, value):
            outs[s] = value

        def ready(s):
            @pl.when(s == me)
            def _():
                item_own().wait()

            @pl.when(s != me)
            def _():
                item_in(s).wait_recv()

        scan_items(get, put, ready, leave_home, wsel[0], wsel[1], *scratch, 32)

    def drain_sends(i, carry):
        @pl.when(i != me)
        def _():
            item_out(i).wait_send()

        return carry

    lax.fori_loop(0, 24, drain_sends, 0)

    @pl.when(me < 24)
    def _():
        leave_home(31)

    mine = (me < 24) & (group == y)

    def drain_items(n, carry):
        local = mine & (n == video * 3 + head)

        @pl.when(local)
        def _():
            home_own().wait()

        @pl.when(jnp.logical_not(local))
        def _():
            home_in(n).wait_recv()

        return carry

    lax.fori_loop(0, 24, drain_items, 0)

    @pl.when(me < 24)
    def _():
        def drain_homes(s, carry):
            @pl.when(jnp.logical_not(stays(s)))
            def _():
                home(s).wait_send()

            return carry

        lax.fori_loop(0, 32, drain_homes, 0)


def run_scan(items, wsel):
    return pl.pallas_call(
        scan_kernel,
        out_shape=jax.ShapeDtypeStruct((8, 192, 128), BF),
        in_specs=[VMEM_SPEC] * 2,
        out_specs=VMEM_SPEC,
        scratch_shapes=[
            pltpu.VMEM((32, 208, 128), BF),
            pltpu.VMEM((32, 64, 128), BF),
            pltpu.SemaphoreType.DMA((24,)),
            pltpu.SemaphoreType.DMA((32,)),
            pltpu.SemaphoreType.DMA((32,)),
            pltpu.SemaphoreType.DMA((24,)),
        ]
        + SCAN_SCRATCH,
        compiler_params=pltpu.CompilerParams(collective_id=1, has_side_effects=True),
        name="ttt_scan",
    )(items, wsel)


def body(attn_query, attn_key, attn_value, prompt_len, ttt_weight, init_w1, init_w2t, step_rate):
    def turned(array):
        return jnp.swapaxes(array, 1, 2)

    items, wsel = gather_project(
        prompt_len,
        turned(attn_query),
        turned(attn_key),
        turned(attn_value),
        ttt_weight.T,
        jnp.swapaxes(step_rate, 0, 1),
        init_w1,
        init_w2t,
    )
    results = run_scan(items, wsel)
    return turned(results)


def solution(mesh):
    in_specs = (
        P(None, "seg", "head"),
        P(None, "seg", "head"),
        P(None, "seg", "head"),
        P(None, "seg"),
        P(None, "head"),
        P("head", None, None),
        P("head", None, None),
        P(None, "head", "seg"),
    )
    return jax.shard_map(
        body, mesh=mesh, in_specs=in_specs, out_specs=P(None, "seg", "head"), check_vma=False
    )
```

```python
import math

import jax
import jax.numpy as jnp
from jax import lax
from jax.experimental import pallas as pl
from jax.experimental.pallas import tpu as pltpu
from jax.sharding import PartitionSpec as P

F32, BF = jnp.float32, jnp.bfloat16
GC = math.sqrt(2.0 / math.pi)
GA = 0.044715
MESH = pl.DeviceIdType.MESH
VMEM_SPEC = pl.BlockSpec(memory_space=pltpu.VMEM)


def nn(a, b):
    return lax.dot_general(a, b, (((1,), (0,)), ((), ())), preferred_element_type=F32)


def nt(a, b):
    return lax.dot_general(a, b, (((1,), (1,)), ((), ())), preferred_element_type=F32)


def tn(a, b):
    return lax.dot_general(a, b, (((0,), (0,)), ((), ())), preferred_element_type=F32)


def attend(q, k, v, length, put):
    position = lax.broadcasted_iota(jnp.int32, (128, 1), 0)
    usable = (position >= 64) | (position < length)
    for h in range(3):
        rows = slice(64 * h, 64 * h + 64)
        scores = tn(k[rows, :], q[rows, :]) * 0.125
        scores = jnp.where(usable, scores, -1e30)
        exponent = jnp.exp(scores - jnp.max(scores, axis=0, keepdims=True))
        weights = (exponent * (1.0 / jnp.sum(exponent, axis=0, keepdims=True))).astype(BF)
        put(h, nn(v[rows, :], weights).astype(BF))


def item_of(video, group, head):
    return (video * 2 + group) * 3 + head


def gather_kernel(
    lengths, q, k, v, wt, rate, w1, w2t, out, wsel,
    buf, pbuf, acc, ssq, wv, wb, rate2,
    wsem, isem, psem, rsem, lsem, recv, csem, ysend, yrecv, xsem, msem, wrecv,
):
    me_h, me_s = lax.axis_index("head"), lax.axis_index("seg")
    z, y = me_h // 2, lax.rem(me_h, 2)
    row, x, core = me_s // 8, lax.rem(me_s // 2, 4), lax.rem(me_s, 2)
    other = 1 - y

    def device(seg, head):
        return {"seg": seg, "head": head}

    right, left = device(me_s, lax.rem(me_h + 2, 16)), device(me_s, lax.rem(me_h + 14, 16))
    partner = device(me_s, 2 * z + other)
    above = device(lax.rem(me_s + 8, 32), 2 * z + lax.rem(y + (row + 1) // 4, 2))
    below = device(lax.rem(me_s + 24, 32), 2 * z + lax.rem(y + (4 - row) // 4, 2))
    xpeer = [device(8 * row + 2 * lax.rem(x + dx, 4) + core, me_h) for dx in (1, 2, 3)]
    mate = device(8 * row + 2 * x + 1 - core, me_h)
    barrier = pltpu.get_barrier_semaphore()
    for peer in (right, left, partner, above, below, mate, *xpeer):
        pl.semaphore_signal(barrier, inc=1, device_id=peer, device_id_type=MESH)
    load = pltpu.make_async_copy(wt, wv, wsem)
    load.start()
    pl.semaphore_wait(barrier, 9)

    def remote(src, dst, send, receive, peer):
        return pltpu.make_async_remote_copy(
            src_ref=src, dst_ref=dst, send_sem=send, recv_sem=receive,
            device_id=peer, device_id_type=MESH,
        )

    item = jnp.minimum(me_s, 23)
    head, group = lax.rem(item, 3), lax.rem(item // 3, 2)

    def start_weight(n):
        source = w1 if n == 0 else w2t
        return remote(source.at[head], wsel.at[n], isem.at[2 + n], isem.at[n], partner)

    def start_local(n):
        source = w1 if n == 0 else w2t
        return pltpu.make_async_copy(source.at[head], wsel.at[n], isem.at[n])

    rates = remote(rate, rate2, isem.at[4], isem.at[5], partner)
    rates.start()

    @pl.when(group == y)
    def _():
        for n in range(2):
            start_local(n).start()
            start_weight(n).start()


    def block(zo, c, yo, sem, peer):
        return remote(buf.at[c, zo, yo], buf.at[c, zo, yo], sem, recv.at[zo, c, yo], peer)

    def to_right(zo, c, yo, d, o):
        return block(zo, c, yo, rsem.at[d, o, c], right)

    def to_left(zo, c, yo, d, o):
        return block(zo, c, yo, lsem.at[d, o, c], left)

    def to_partner(c):
        return remote(pbuf.at[c], buf.at[c, z, y], psem.at[c], recv.at[z, c, y], partner)

    zc = 2 * x + core
    lanes = pl.ds(pl.multiple_of(zc * 384, 128), 384)

    def half_of(chunk, g):
        columns = pl.ds(pl.multiple_of(chunk * 384, 128), 384)
        return wb.at[pl.ds(pl.multiple_of(288 * g, 32), 288), columns]

    def cross(g, peer):
        source = wt.at[pl.ds(288 * g, 288), lanes]
        return remote(source, half_of(zc, g), csem, yrecv.at[g], peer)

    def onward(g):
        peer = device(lax.rem(me_s + 8 + 16 * g, 32), me_h)
        return remote(half_of(zc, g), half_of(zc, g), ysend.at[g], yrecv.at[g], peer)

    def weight(chunk, g, sem, peer):
        return remote(half_of(chunk, g), half_of(chunk, g), sem, wrecv.at[chunk, g], peer)

    def chunk_at(dx):
        return 2 * lax.rem(x + dx, 4) + core

    def to_mate(dx, g):
        return weight(chunk_at(dx), g, msem.at[dx, g], mate)

    def spread(g):
        for dx in (1, 3, 2):
            weight(zc, g, xsem.at[dx - 1, g], xpeer[dx - 1]).start()
        to_mate(0, g).start()

    sooner = row // 2
    later = 1 - sooner
    edge = (row == 0) | (row == 3)

    def attend_pair(pair, put_half):
        for half in range(2):
            video = 2 * pair + half

            def put(h, value):
                put_half(slice(64 * h, 64 * h + 64), slice(128 * half, 128 * half + 128), value)

            attend(q[video], k[video], v[video], lengths[0, video], put)

    def hop(d, o, c):
        yo = y if o == 0 else other
        zr, zl = lax.rem(z + 8 - d, 8), lax.rem(z + d, 8)
        if d < 4 or c == 0:
            to_right(zr, c, yo, 0, 0).wait_recv()
        if d < 3 or (d == 3 and c == 0):
            to_right(zr, c, yo, d, o).start()
        if d < 4 or c == 1:
            to_left(zl, c, yo, 0, 0).wait_recv()
        if d < 3 or (d == 3 and c == 1):
            to_left(zl, c, yo, d, o).start()

    def send_own(c):
        to_right(z, c, y, 0, 0).start()
        to_left(z, c, y, 0, 0).start()

    def take_partner(c):
        block(z, c, other, psem.at[c], partner).wait_recv()
        to_right(z, c, other, 0, 1).start()
        to_left(z, c, other, 0, 1).start()

    @pl.when(row == 3)
    def _():
        cross(0, above).start()

    @pl.when(row == 0)
    def _():
        cross(1, below).start()

    def attend_partner(c, carry):
        def put_half(rows, cols, value):
            pbuf[c, rows, cols] = value

        attend_pair(2 * other + c, put_half)

        @pl.when(c == 1)
        def _():
            to_partner(0).start()

        return carry

    lax.fori_loop(0, 2, attend_partner, 0)

    def attend_own(c, carry):
        def put_half(rows, cols, value):
            buf[c, z, y, rows, cols] = value

        attend_pair(2 * y + c, put_half)

        @pl.when(c == 0)
        def _():
            to_partner(1).start()

            @pl.when(edge)
            def _():
                onward(sooner).wait_recv()
                onward(sooner).start()
                spread(sooner)

        @pl.when(c == 1)
        def _():
            send_own(0)

        return carry

    lax.fori_loop(0, 2, attend_own, 0)
    load.wait()
    acc[...] = jnp.zeros((2, 2, 576, 256), F32)
    send_own(1)
    hop(1, 0, 0)
    hop(1, 0, 1)

    @pl.when(jnp.logical_not(edge))
    def _():
        onward(sooner).wait_recv()
        onward(sooner).start()
        spread(sooner)

    hop(2, 0, 0)
    take_partner(0)
    hop(2, 0, 1)

    @pl.when(jnp.logical_not(edge))
    def _():
        onward(later).wait_recv()
        onward(later).start()
        spread(later)

    hop(3, 0, 0)
    hop(1, 1, 0)
    hop(3, 0, 1)
    take_partner(1)
    hop(2, 1, 0)

    @pl.when(edge)
    def _():
        onward(later).wait_recv()
        spread(later)

    hop(1, 1, 1)
    for dx in (1, 3, 2):
        weight(chunk_at(dx), sooner, csem, mate).wait_recv()
        to_mate(dx, sooner).start()
    hop(3, 1, 0)
    hop(2, 1, 1)
    hop(4, 0, 0)
    hop(4, 1, 0)

    def project_own(c):
        xb = buf[c].reshape(3072, 256)
        acc[0, c] = nn(wv[...], xb)
        xf = xb.astype(F32)
        ssq[c] = jnp.sum((xf * xf).reshape(384, 8, 256), axis=0)

    project_own(0)
    hop(3, 1, 1)
    for dx in (1, 3, 2):
        weight(chunk_at(dx), later, csem, mate).wait_recv()
        to_mate(dx, later).start()
    hop(4, 0, 1)
    hop(4, 1, 1)
    project_own(1)
    for n in range(4):
        for g in range(2):
            weight(2 * n + 1 - core, g, csem, mate).wait_recv()

    def project_other(c, carry):
        acc[1, c] = nn(wb[...], buf[c].reshape(3072, 256))
        return carry

    lax.fori_loop(0, 2, project_other, 0)
    rates.wait_recv()
    position = lax.broadcasted_iota(jnp.int32, (1, 128), 1)

    def finish(c, carry):
        mean = jnp.sum(ssq[c], axis=0, keepdims=True) * (1.0 / 3072.0)
        scale = lax.rsqrt(mean + 1e-6)
        for g in range(2):
            projected = (acc[g, c] * scale).astype(BF)
            source_rate = rate if g == 0 else rate2
            for half in range(2):
                video = 4 * y + 2 * c + half
                usable = (position >= 64) | (position < lengths[0, video])
                for h in range(3):
                    slot = item_of(2 * c + half, y if g == 0 else other, h)
                    out[slot, 0:192, :] = projected[
                        192 * h : 192 * h + 192, 128 * half : 128 * half + 128
                    ]
                    eta = jnp.where(usable, source_rate[h, pl.ds(video, 1), :], 0.0)
                    out[slot, 192:208, :] = jnp.broadcast_to(eta, (16, 128)).astype(BF)
        return carry

    lax.fori_loop(0, 2, finish, 0)


    rates.wait_send()

    @pl.when(group == y)
    def _():
        for n in range(2):
            start_local(n).wait()
            start_weight(n).wait_send()

    @pl.when(group != y)
    def _():
        for n in range(2):
            start_weight(n).wait_recv()

    @pl.when(edge)
    def _():
        cross(0, above).wait_send()

    onward(sooner).wait_send()

    @pl.when(jnp.logical_not(edge))
    def _():
        onward(later).wait_send()

    for g in range(2):
        for dx in range(4):
            to_mate(dx, g).wait_send()
        for dx in range(3):
            weight(zc, g, xsem.at[dx, g], xpeer[dx]).wait_send()

    def drain(c, carry):
        to_partner(c).wait_send()
        for o in range(2):
            for d in range(3):
                to_right(z, c, y, d, o).wait_send()
                to_left(z, c, y, d, o).wait_send()

            @pl.when(c == 0)
            def _():
                to_right(z, c, y, 3, o).wait_send()

            @pl.when(c == 1)
            def _():
                to_left(z, c, y, 3, o).wait_send()

        return carry

    lax.fori_loop(0, 2, drain, 0)


def gather_project(lengths, q, k, v, wt, rate, w1, w2t):
    any_spec = pl.BlockSpec(memory_space=pl.ANY)
    dma = pltpu.SemaphoreType.DMA
    return pl.pallas_call(
        gather_kernel,
        out_shape=(
            jax.ShapeDtypeStruct((24, 208, 128), BF),
            jax.ShapeDtypeStruct((2, 64, 256), F32),
        ),
        in_specs=[
            pl.BlockSpec(memory_space=pltpu.SMEM),
            VMEM_SPEC,
            VMEM_SPEC,
            VMEM_SPEC,
            any_spec,
            VMEM_SPEC,
            VMEM_SPEC,
            VMEM_SPEC,
        ],
        out_specs=(VMEM_SPEC, VMEM_SPEC),
        scratch_shapes=[
            pltpu.VMEM((2, 8, 2, 192, 256), BF),
            pltpu.VMEM((2, 192, 256), BF),
            pltpu.VMEM((2, 2, 576, 256), F32),
            pltpu.VMEM((2, 8, 256), F32),
            pltpu.VMEM((576, 3072), BF),
            pltpu.VMEM((576, 3072), BF),
            pltpu.VMEM((3, 8, 128), F32),
            dma,
            dma((6,)),
            dma((2,)),
            dma((4, 2, 2)),
            dma((4, 2, 2)),
            dma((8, 2, 2)),
            dma,
            dma((2,)),
            dma((2,)),
            dma((3, 2)),
            dma((4, 2)),
            dma((8, 2)),
        ],
        compiler_params=pltpu.CompilerParams(
            collective_id=0, has_side_effects=True, vmem_limit_bytes=56 << 20
        ),
        name="attend_gather_project",
    )(lengths, q, k, v, wt, rate, w1, w2t)


def forward(u, w2b, xt, st):
    sq = u * u
    t = jnp.tanh(u * (GC + (GC * GA) * sq))
    half = 0.5 + 0.5 * t
    hb = (u * half).astype(BF)
    z = nn(w2b, hb)
    center = z - jnp.mean(z, axis=0, keepdims=True)
    rs = lax.rsqrt(jnp.mean(center * center, axis=0, keepdims=True) + 1e-5)
    y = center * rs
    return sq, t, half, hb, rs, y, y + (xt - st)


def scan_items(get, put, ready, leave, w10, w2t0, w1s, w2s, w2ts, ub, xs, rprev, count):
    left = lax.broadcasted_iota(jnp.int32, (64, 128), 1) < 64
    left1 = lax.broadcasted_iota(jnp.int32, (1, 128), 1) < 64
    zero = jnp.zeros((64, 128), F32)
    zero1 = jnp.zeros((1, 128), F32)
    w1s[...] = w10.T
    w2s[...] = w2t0
    w2ts[...] = w2t0.T
    ready(0)
    x0 = jnp.where(left, get(0, 64, 64), zero)
    ub[...] = nn(w1s[...].astype(BF), x0.astype(BF))
    xs[...] = x0.T.astype(BF)

    def step(xt, st, eta, xnt):
        xntb = xnt.astype(BF)
        u = ub[...]
        sq, t, half, hb, rs, y, r = forward(u, w2s[...].astype(BF), xt, st)
        dy = r * (eta * (1.0 / 64.0))
        m1 = jnp.mean(dy, axis=0, keepdims=True)
        m2 = jnp.mean(dy * y, axis=0, keepdims=True)
        dzb = (rs * (dy - m1 - y * m2)).astype(BF)
        slope = half + (0.5 * u) * ((1.0 - t * t) * (GC + (3.0 * GC * GA) * sq))
        dub = (nn(w2ts[...].astype(BF), dzb) * slope).astype(BF)
        x = xs[...]
        w1 = w1s[...]
        ub[...] = nn(w1.astype(BF), xntb) - nn(dub, nn(x, xntb).astype(BF))
        w1s[...] = w1 - nn(dub, x)
        w2s[...] -= nt(dzb, hb)
        w2ts[...] -= nt(hb, dzb)
        xs[...] = xnt.T.astype(BF)
        return r

    def segment(s, carry):
        prev = jnp.maximum(s - 1, 0)

        @pl.when(s + 1 < count)
        def _():
            ready(s + 1)

        qs, ks, vs = get(s, 0, 64), get(s, 64, 64), get(s, 128, 64)
        qp = get(prev, 0, 64)
        kn = get(jnp.minimum(s + 1, count - 1), 64, 64)
        rate = get(s, 192, 1)
        mid = jnp.where(left, qs, ks)
        even = step(
            jnp.where(left, ks, qp), jnp.where(left, vs, zero), jnp.where(left1, rate, zero1), mid
        )
        put(prev, jnp.where(left, rprev[...], even).astype(BF))
        rprev[...] = step(
            mid, jnp.where(left, zero, vs), jnp.where(left1, zero1, rate), jnp.where(left, kn, qs)
        )

        @pl.when(s > 0)
        def _():
            leave(prev)

        return carry

    rprev[...] = zero
    lax.fori_loop(0, count, segment, 0)
    last = forward(ub[...], w2s[...].astype(BF), get(count - 1, 0, 64), zero)[-1]
    put(count - 1, jnp.where(left, rprev[...], last).astype(BF))


SCAN_SCRATCH = [
    pltpu.VMEM((256, 64), F32),
    pltpu.VMEM((64, 256), F32),
    pltpu.VMEM((256, 64), F32),
    pltpu.VMEM((256, 128), F32),
    pltpu.VMEM((128, 64), BF),
    pltpu.VMEM((64, 128), F32),
]


def scan_kernel(items, wsel, res, qkv, outs, isem, qsem, osem, rsem, *scratch):
    me, me_h = lax.axis_index("seg"), lax.axis_index("head")
    z, y = me_h // 2, lax.rem(me_h, 2)
    barrier = pltpu.get_barrier_semaphore()

    def greet(k, carry):
        peer = lax.rem(me + k, 32)
        pl.semaphore_signal(
            barrier, inc=1, device_id={"seg": peer, "head": me_h}, device_id_type=MESH
        )
        pl.semaphore_signal(
            barrier, inc=1, device_id={"seg": peer, "head": 2 * z + 1 - y}, device_id_type=MESH
        )
        return carry

    lax.fori_loop(1, 32, greet, 0)
    pl.semaphore_signal(
        barrier, inc=1, device_id={"seg": me, "head": 2 * z + 1 - y}, device_id_type=MESH
    )
    pl.semaphore_wait(barrier, 63)

    def item_out(i):
        return pltpu.make_async_remote_copy(
            src_ref=items.at[i],
            dst_ref=qkv.at[me],
            send_sem=isem.at[i],
            recv_sem=qsem.at[me],
            device_id={"seg": i, "head": me_h},
            device_id_type=MESH,
        )

    def item_in(s):
        return pltpu.make_async_remote_copy(
            src_ref=items.at[0],
            dst_ref=qkv.at[s],
            send_sem=isem.at[0],
            recv_sem=qsem.at[s],
            device_id={"seg": s, "head": me_h},
            device_id_type=MESH,
        )

    own = jnp.minimum(me, 23)
    video, group, head = 4 * y + own // 6, lax.rem(own // 3, 2), lax.rem(own, 3)

    def place(v, h):
        return res.at[v, pl.ds(pl.multiple_of(64 * h, 64), 64), :]

    def item_own():
        return pltpu.make_async_copy(items.at[own], qkv.at[own], qsem.at[own])

    def home(s):
        return pltpu.make_async_remote_copy(
            src_ref=outs.at[s],
            dst_ref=place(video, head),
            send_sem=osem.at[s],
            recv_sem=rsem.at[video * 3 + head],
            device_id={"seg": s, "head": 2 * z + group},
            device_id_type=MESH,
        )

    def home_own():
        return pltpu.make_async_copy(outs.at[own], place(video, head), rsem.at[video * 3 + head])

    def home_in(n):
        return pltpu.make_async_remote_copy(
            src_ref=outs.at[0],
            dst_ref=place(n // 3, lax.rem(n, 3)),
            send_sem=osem.at[0],
            recv_sem=rsem.at[n],
            device_id={"seg": me, "head": 2 * z + 1 - y},
            device_id_type=MESH,
        )

    def stays(s):
        return (s == me) & (group == y)

    @pl.when(me < 24)
    def _():
        item_own().start()

    def send(k, carry):
        i = lax.rem(me + k, 24)

        @pl.when(i != me)
        def _():
            item_out(i).start()

        return carry

    lax.fori_loop(0, 24, send, 0)

    def leave_home(s):
        @pl.when(stays(s))
        def _():
            home_own().start()

        @pl.when(jnp.logical_not(stays(s)))
        def _():
            home(s).start()

    @pl.when(me < 24)
    def _():
        def get(s, row, rows):
            return qkv[s, row : row + rows, :].astype(F32)

        def put(s, value):
            outs[s] = value

        def ready(s):
            @pl.when(s == me)
            def _():
                item_own().wait()

            @pl.when(s != me)
            def _():
                item_in(s).wait_recv()

        scan_items(get, put, ready, leave_home, wsel[0], wsel[1], *scratch, 32)

    def drain_sends(i, carry):
        @pl.when(i != me)
        def _():
            item_out(i).wait_send()

        return carry

    lax.fori_loop(0, 24, drain_sends, 0)

    @pl.when(me < 24)
    def _():
        leave_home(31)

    mine = (me < 24) & (group == y)

    def drain_items(n, carry):
        local = mine & (n == video * 3 + head)

        @pl.when(local)
        def _():
            home_own().wait()

        @pl.when(jnp.logical_not(local))
        def _():
            home_in(n).wait_recv()

        return carry

    lax.fori_loop(0, 24, drain_items, 0)

    @pl.when(me < 24)
    def _():
        def drain_homes(s, carry):
            @pl.when(jnp.logical_not(stays(s)))
            def _():
                home(s).wait_send()

            return carry

        lax.fori_loop(0, 32, drain_homes, 0)


def run_scan(items, wsel):
    return pl.pallas_call(
        scan_kernel,
        out_shape=jax.ShapeDtypeStruct((8, 192, 128), BF),
        in_specs=[VMEM_SPEC] * 2,
        out_specs=VMEM_SPEC,
        scratch_shapes=[
            pltpu.VMEM((32, 208, 128), BF),
            pltpu.VMEM((32, 64, 128), BF),
            pltpu.SemaphoreType.DMA((24,)),
            pltpu.SemaphoreType.DMA((32,)),
            pltpu.SemaphoreType.DMA((32,)),
            pltpu.SemaphoreType.DMA((24,)),
        ]
        + SCAN_SCRATCH,
        compiler_params=pltpu.CompilerParams(collective_id=1, has_side_effects=True),
        name="ttt_scan",
    )(items, wsel)


def body(attn_query, attn_key, attn_value, prompt_len, ttt_weight, init_w1, init_w2t, step_rate):
    def turned(array):
        return jnp.swapaxes(array, 1, 2)

    items, wsel = gather_project(
        jnp.swapaxes(prompt_len, 0, 1),
        turned(attn_query),
        turned(attn_key),
        turned(attn_value),
        ttt_weight.T,
        jnp.swapaxes(step_rate, 0, 1),
        init_w1,
        init_w2t,
    )
    results = run_scan(items, wsel)
    return turned(results)


def solution(mesh):
    in_specs = (
        P(None, "seg", "head"),
        P(None, "seg", "head"),
        P(None, "seg", "head"),
        P(None, "seg"),
        P(None, "head"),
        P("head", None, None),
        P("head", None, None),
        P(None, "head", "seg"),
    )
    return jax.shard_map(
        body, mesh=mesh, in_specs=in_specs, out_specs=P(None, "seg", "head"), check_vma=False
    )
```

```python
import math

import jax
import jax.numpy as jnp
from jax import lax
from jax.experimental import pallas as pl
from jax.experimental.pallas import tpu as pltpu
from jax.sharding import PartitionSpec as P

F32, BF = jnp.float32, jnp.bfloat16
GC = math.sqrt(2.0 / math.pi)
GA = 0.044715
MESH = pl.DeviceIdType.MESH
VMEM_SPEC = pl.BlockSpec(memory_space=pltpu.VMEM)


def nn(a, b):
    return lax.dot_general(a, b, (((1,), (0,)), ((), ())), preferred_element_type=F32)


def nt(a, b):
    return lax.dot_general(a, b, (((1,), (1,)), ((), ())), preferred_element_type=F32)


def tn(a, b):
    return lax.dot_general(a, b, (((0,), (0,)), ((), ())), preferred_element_type=F32)


def attend(q, k, v, length, put):
    position = lax.broadcasted_iota(jnp.int32, (128, 1), 0)
    usable = (position >= 64) | (position < length)
    for h in range(3):
        rows = slice(64 * h, 64 * h + 64)
        scores = tn(k[rows, :], q[rows, :]) * 0.125
        scores = jnp.where(usable, scores, -1e30)
        exponent = jnp.exp(scores - jnp.max(scores, axis=0, keepdims=True))
        weights = (exponent * (1.0 / jnp.sum(exponent, axis=0, keepdims=True))).astype(BF)
        put(h, nn(v[rows, :], weights).astype(BF))


def forward(u, w2b, xt, st):
    sq = u * u
    t = jnp.tanh(u * (GC + (GC * GA) * sq))
    half = 0.5 + 0.5 * t
    hb = (u * half).astype(BF)
    z = nn(w2b, hb)
    center = z - jnp.mean(z, axis=0, keepdims=True)
    rs = lax.rsqrt(jnp.mean(center * center, axis=0, keepdims=True) + 1e-5)
    y = center * rs
    return sq, t, half, hb, rs, y, y + (xt - st)


def scan_items(get, put, ready, leave, w10, w2t0, w1s, w2s, w2ts, ub, xs, rprev, count):
    left = lax.broadcasted_iota(jnp.int32, (64, 128), 1) < 64
    left1 = lax.broadcasted_iota(jnp.int32, (1, 128), 1) < 64
    zero = jnp.zeros((64, 128), F32)
    zero1 = jnp.zeros((1, 128), F32)
    w1s[...] = w10.T
    w2s[...] = w2t0
    w2ts[...] = w2t0.T
    ready(0)
    x0 = jnp.where(left, get(0, 64, 64), zero)
    ub[...] = nn(w1s[...].astype(BF), x0.astype(BF))
    xs[...] = x0.T.astype(BF)

    def step(xt, st, eta, xnt):
        xntb = xnt.astype(BF)
        u = ub[...]
        sq, t, half, hb, rs, y, r = forward(u, w2s[...].astype(BF), xt, st)
        dy = r * (eta * (1.0 / 64.0))
        m1 = jnp.mean(dy, axis=0, keepdims=True)
        m2 = jnp.mean(dy * y, axis=0, keepdims=True)
        dzb = (rs * (dy - m1 - y * m2)).astype(BF)
        slope = half + (0.5 * u) * ((1.0 - t * t) * (GC + (3.0 * GC * GA) * sq))
        dub = (nn(w2ts[...].astype(BF), dzb) * slope).astype(BF)
        x = xs[...]
        w1 = w1s[...]
        ub[...] = nn(w1.astype(BF), xntb) - nn(dub, nn(x, xntb).astype(BF))
        w1s[...] = w1 - nn(dub, x)
        w2s[...] -= nt(dzb, hb)
        w2ts[...] -= nt(hb, dzb)
        xs[...] = xnt.T.astype(BF)
        return r

    def segment(s, carry):
        prev = jnp.maximum(s - 1, 0)

        @pl.when(s + 1 < count)
        def _():
            ready(s + 1)

        qs, ks, vs = get(s, 0, 64), get(s, 64, 64), get(s, 128, 64)
        qp = get(prev, 0, 64)
        kn = get(jnp.minimum(s + 1, count - 1), 64, 64)
        rate = get(s, 192, 1)
        mid = jnp.where(left, qs, ks)
        even = step(
            jnp.where(left, ks, qp), jnp.where(left, vs, zero), jnp.where(left1, rate, zero1), mid
        )
        put(prev, jnp.where(left, rprev[...], even).astype(BF))
        rprev[...] = step(
            mid, jnp.where(left, zero, vs), jnp.where(left1, zero1, rate), jnp.where(left, kn, qs)
        )

        @pl.when(s > 0)
        def _():
            leave(prev)

        return carry

    rprev[...] = zero
    lax.fori_loop(0, count, segment, 0)
    last = forward(ub[...], w2s[...].astype(BF), get(count - 1, 0, 64), zero)[-1]
    put(count - 1, jnp.where(left, rprev[...], last).astype(BF))


SCAN_SCRATCH = [
    pltpu.VMEM((256, 64), F32),
    pltpu.VMEM((64, 256), F32),
    pltpu.VMEM((256, 64), F32),
    pltpu.VMEM((256, 128), F32),
    pltpu.VMEM((128, 64), BF),
    pltpu.VMEM((64, 128), F32),
]


def fused_kernel(
    lengths, q, k, v, wt, rate, w1, w2t, res,
    items, wsel, qkv, outs, ssend, qsem, osem, hsem,
    buf, pbuf, acc, ssq, wv, wb, rate2,
    wsem, isem, psem, rsem, lsem, recv, csem, ysend, yrecv, xsem, msem, wrecv, *scratch,
):
    me_h, me_s = lax.axis_index("head"), lax.axis_index("seg")
    z, y = me_h // 2, lax.rem(me_h, 2)
    row, x, core = me_s // 8, lax.rem(me_s // 2, 4), lax.rem(me_s, 2)
    other = 1 - y

    def device(seg, head):
        return {"seg": seg, "head": head}

    right, left = device(me_s, lax.rem(me_h + 2, 16)), device(me_s, lax.rem(me_h + 14, 16))
    partner = device(me_s, 2 * z + other)
    above = device(lax.rem(me_s + 8, 32), 2 * z + lax.rem(y + (row + 1) // 4, 2))
    below = device(lax.rem(me_s + 24, 32), 2 * z + lax.rem(y + (4 - row) // 4, 2))
    xpeer = [device(8 * row + 2 * lax.rem(x + dx, 4) + core, me_h) for dx in (1, 2, 3)]
    mate = device(8 * row + 2 * x + 1 - core, me_h)
    barrier = pltpu.get_barrier_semaphore()

    def greet(n, carry):
        peer = lax.rem(me_s + n, 32)
        for target in (device(peer, me_h), device(peer, 2 * z + other)):
            pl.semaphore_signal(barrier, inc=1, device_id=target, device_id_type=MESH)
        return carry

    lax.fori_loop(1, 32, greet, 0)
    for target in (right, left, partner):
        pl.semaphore_signal(barrier, inc=1, device_id=target, device_id_type=MESH)
    load = pltpu.make_async_copy(wt, wv, wsem)
    load.start()
    pl.semaphore_wait(barrier, 65)

    def remote(src, dst, send, receive, peer):
        return pltpu.make_async_remote_copy(
            src_ref=src, dst_ref=dst, send_sem=send, recv_sem=receive,
            device_id=peer, device_id_type=MESH,
        )

    me = me_s
    own = jnp.minimum(me, 23)
    borrowed = own < 12
    video, head = 4 * y + lax.rem(own, 12) // 3, lax.rem(own, 3)
    group = lax.rem(y + 1 - own // 12, 2)

    def start_weight(n):
        source = w1 if n == 0 else w2t
        return remote(source.at[head], wsel.at[n], isem.at[2 + n], isem.at[n], partner)

    def start_local(n):
        source = w1 if n == 0 else w2t
        return pltpu.make_async_copy(source.at[head], wsel.at[n], isem.at[n])

    rates = remote(rate, rate2, isem.at[4], isem.at[5], partner)
    rates.start()

    for n in range(2):

        @pl.when(borrowed)
        def _():
            start_weight(n).start()

        @pl.when(jnp.logical_not(borrowed))
        def _():
            start_local(n).start()


    def block(zo, c, yo, sem, peer):
        return remote(buf.at[c, zo, yo], buf.at[c, zo, yo], sem, recv.at[zo, c, yo], peer)

    def to_right(zo, c, yo, d, o):
        return block(zo, c, yo, rsem.at[d, o, c], right)

    def to_left(zo, c, yo, d, o):
        return block(zo, c, yo, lsem.at[d, o, c], left)

    def to_partner(c):
        return remote(pbuf.at[c], buf.at[c, z, y], psem.at[c], recv.at[z, c, y], partner)

    zc = 2 * x + core
    lanes = pl.ds(pl.multiple_of(zc * 384, 128), 384)

    def half_of(chunk, g):
        columns = pl.ds(pl.multiple_of(chunk * 384, 128), 384)
        return wb.at[pl.ds(pl.multiple_of(288 * g, 32), 288), columns]

    def cross(g, peer):
        source = wt.at[pl.ds(288 * g, 288), lanes]
        return remote(source, half_of(zc, g), csem, yrecv.at[g], peer)

    def onward(g):
        peer = device(lax.rem(me_s + 8 + 16 * g, 32), me_h)
        return remote(half_of(zc, g), half_of(zc, g), ysend.at[g], yrecv.at[g], peer)

    def weight(chunk, g, sem, peer):
        return remote(half_of(chunk, g), half_of(chunk, g), sem, wrecv.at[chunk, g], peer)

    def chunk_at(dx):
        return 2 * lax.rem(x + dx, 4) + core

    def to_mate(dx, g):
        return weight(chunk_at(dx), g, msem.at[dx, g], mate)

    def spread(g):
        for dx in (1, 3, 2):
            weight(zc, g, xsem.at[dx - 1, g], xpeer[dx - 1]).start()
        to_mate(0, g).start()

    sooner = row // 2
    later = 1 - sooner
    edge = (row == 0) | (row == 3)

    def attend_pair(pair, put_half):
        for half in range(2):
            video = 2 * pair + half

            def put(h, value):
                put_half(slice(64 * h, 64 * h + 64), slice(128 * half, 128 * half + 128), value)

            attend(q[video], k[video], v[video], lengths[0, video], put)

    def hop(d, o, c):
        yo = y if o == 0 else other
        zr, zl = lax.rem(z + 8 - d, 8), lax.rem(z + d, 8)
        if d < 4 or c == 0:
            to_right(zr, c, yo, 0, 0).wait_recv()
        if d < 3 or (d == 3 and c == 0):
            to_right(zr, c, yo, d, o).start()
        if d < 4 or c == 1:
            to_left(zl, c, yo, 0, 0).wait_recv()
        if d < 3 or (d == 3 and c == 1):
            to_left(zl, c, yo, d, o).start()

    def send_own(c):
        to_right(z, c, y, 0, 0).start()
        to_left(z, c, y, 0, 0).start()

    def take_partner(c):
        block(z, c, other, psem.at[c], partner).wait_recv()
        to_right(z, c, other, 0, 1).start()
        to_left(z, c, other, 0, 1).start()

    @pl.when(row == 3)
    def _():
        cross(0, above).start()

    @pl.when(row == 0)
    def _():
        cross(1, below).start()

    def attend_partner(c, carry):
        def put_half(rows, cols, value):
            pbuf[c, rows, cols] = value

        attend_pair(2 * other + c, put_half)

        @pl.when(c == 1)
        def _():
            to_partner(0).start()

        return carry

    lax.fori_loop(0, 2, attend_partner, 0)

    def attend_own(c, carry):
        def put_half(rows, cols, value):
            buf[c, z, y, rows, cols] = value

        attend_pair(2 * y + c, put_half)

        @pl.when(c == 0)
        def _():
            to_partner(1).start()

            @pl.when(edge)
            def _():
                onward(sooner).wait_recv()
                onward(sooner).start()
                spread(sooner)

        @pl.when(c == 1)
        def _():
            send_own(0)

        return carry

    lax.fori_loop(0, 2, attend_own, 0)
    load.wait()
    acc[...] = jnp.zeros((2, 2, 576, 256), F32)
    send_own(1)
    hop(1, 0, 0)
    hop(1, 0, 1)

    @pl.when(jnp.logical_not(edge))
    def _():
        onward(sooner).wait_recv()
        onward(sooner).start()
        spread(sooner)

    hop(2, 0, 0)
    take_partner(0)
    hop(2, 0, 1)

    @pl.when(jnp.logical_not(edge))
    def _():
        onward(later).wait_recv()
        onward(later).start()
        spread(later)

    hop(3, 0, 0)
    hop(1, 1, 0)
    hop(3, 0, 1)
    take_partner(1)
    hop(2, 1, 0)

    @pl.when(edge)
    def _():
        onward(later).wait_recv()
        spread(later)

    hop(1, 1, 1)
    for dx in (1, 3, 2):
        weight(chunk_at(dx), sooner, csem, mate).wait_recv()
        to_mate(dx, sooner).start()
    hop(3, 1, 0)
    hop(2, 1, 1)
    hop(4, 0, 0)
    hop(4, 1, 0)

    def item_out(i):
        return pltpu.make_async_remote_copy(
            src_ref=items.at[i],
            dst_ref=qkv.at[me],
            send_sem=ssend.at[i],
            recv_sem=qsem.at[me],
            device_id={"seg": i, "head": me_h},
            device_id_type=MESH,
        )

    def item_in(s):
        return pltpu.make_async_remote_copy(
            src_ref=items.at[0],
            dst_ref=qkv.at[s],
            send_sem=ssend.at[0],
            recv_sem=qsem.at[s],
            device_id={"seg": s, "head": me_h},
            device_id_type=MESH,
        )

    def place(v, h):
        return res.at[v, pl.ds(pl.multiple_of(64 * h, 64), 64), :]

    def item_own():
        return pltpu.make_async_copy(items.at[own], qkv.at[own], qsem.at[own])

    def home(s):
        return pltpu.make_async_remote_copy(
            src_ref=outs.at[s],
            dst_ref=place(video, head),
            send_sem=osem.at[s],
            recv_sem=hsem.at[video * 3 + head],
            device_id={"seg": s, "head": 2 * z + group},
            device_id_type=MESH,
        )

    def home_own():
        return pltpu.make_async_copy(outs.at[own], place(video, head), hsem.at[video * 3 + head])

    def home_in(n):
        return pltpu.make_async_remote_copy(
            src_ref=outs.at[0],
            dst_ref=place(n // 3, lax.rem(n, 3)),
            send_sem=osem.at[0],
            recv_sem=hsem.at[n],
            device_id={"seg": me, "head": 2 * z + 1 - y},
            device_id_type=MESH,
        )

    def stays(s):
        return (s == me) & (group == y)

    position = lax.broadcasted_iota(jnp.int32, (1, 128), 1)

    def finish(g, c):
        mean = jnp.sum(ssq[c], axis=0, keepdims=True) * (1.0 / 3072.0)
        projected = (acc[g, c] * lax.rsqrt(mean + 1e-6)).astype(BF)
        source_rate = rate if g == 0 else rate2
        for half in range(2):
            at = 4 * y + 2 * c + half
            usable = (position >= 64) | (position < lengths[0, at])
            for h in range(3):
                slot = (12 if g == 0 else 0) + (2 * c + half) * 3 + h
                items[slot, 0:192, :] = projected[
                    192 * h : 192 * h + 192, 128 * half : 128 * half + 128
                ]
                eta = jnp.where(usable, source_rate[h, pl.ds(at, 1), :], 0.0)
                items[slot, 192:208, :] = jnp.broadcast_to(eta, (16, 128)).astype(BF)

    def send_items(g, c):
        def send(n, carry):
            i = (12 if g == 0 else 0) + 6 * c + lax.rem(me + n, 6)

            @pl.when(i != me)
            def _():
                item_out(i).start()

            @pl.when(i == me)
            def _():
                item_own().start()

            return carry

        lax.fori_loop(0, 6, send, 0)

    def project_own(c):
        xb = buf[c].reshape(3072, 256)
        acc[0, c] = nn(wv[...], xb)
        xf = xb.astype(F32)
        ssq[c] = jnp.sum((xf * xf).reshape(384, 8, 256), axis=0)

    def project_other(c):
        acc[1, c] = nn(wb[...], buf[c].reshape(3072, 256))

    project_own(0)
    finish(0, 0)
    hop(3, 1, 1)
    for dx in (1, 3, 2):
        weight(chunk_at(dx), later, csem, mate).wait_recv()
        to_mate(dx, later).start()
    send_items(0, 0)
    hop(4, 0, 1)
    hop(4, 1, 1)
    project_own(1)
    finish(0, 1)
    rates.wait_recv()
    for n in range(4):
        for g in range(2):
            weight(2 * n + 1 - core, g, csem, mate).wait_recv()
        if n == 0:
            send_items(0, 1)
    project_other(0)
    finish(1, 0)
    project_other(1)
    send_items(1, 0)
    finish(1, 1)


    def drain(c, carry):
        to_partner(c).wait_send()
        for o in range(2):
            for d in range(3):
                to_right(z, c, y, d, o).wait_send()
                to_left(z, c, y, d, o).wait_send()

            @pl.when(c == 0)
            def _():
                to_right(z, c, y, 3, o).wait_send()

            @pl.when(c == 1)
            def _():
                to_left(z, c, y, 3, o).wait_send()

        return carry

    lax.fori_loop(0, 2, drain, 0)
    send_items(1, 1)

    for n in range(2):

        @pl.when(borrowed)
        def _():
            start_weight(n).wait_recv()

        @pl.when(jnp.logical_not(borrowed))
        def _():
            start_local(n).wait()

    def leave_home(s):
        @pl.when(stays(s))
        def _():
            home_own().start()

        @pl.when(jnp.logical_not(stays(s)))
        def _():
            home(s).start()

    @pl.when(me < 24)
    def _():
        def get(s, row, rows):
            return qkv[s, row : row + rows, :].astype(F32)

        def put(s, value):
            outs[s] = value

        def ready(s):
            @pl.when(s == me)
            def _():
                item_own().wait()

            @pl.when(s != me)
            def _():
                item_in(s).wait_recv()

        scan_items(get, put, ready, leave_home, wsel[0], wsel[1], *scratch, 32)

    def drain_sends(i, carry):
        @pl.when(i != me)
        def _():
            item_out(i).wait_send()

        return carry

    lax.fori_loop(0, 24, drain_sends, 0)

    @pl.when(me < 24)
    def _():
        leave_home(31)

    mine = (me < 24) & (group == y)

    def drain_items(n, carry):
        local = mine & (n == video * 3 + head)

        @pl.when(local)
        def _():
            home_own().wait()

        @pl.when(jnp.logical_not(local))
        def _():
            home_in(n).wait_recv()

        return carry

    lax.fori_loop(0, 24, drain_items, 0)

    @pl.when(me < 24)
    def _():
        def drain_homes(s, carry):
            @pl.when(jnp.logical_not(stays(s)))
            def _():
                home(s).wait_send()

            return carry

        lax.fori_loop(0, 32, drain_homes, 0)

    rates.wait_send()

    for n in range(2):

        @pl.when(borrowed)
        def _():
            start_weight(n).wait_send()

    @pl.when(edge)
    def _():
        cross(0, above).wait_send()

    onward(sooner).wait_send()

    @pl.when(jnp.logical_not(edge))
    def _():
        onward(later).wait_send()

    for g in range(2):
        for dx in range(4):
            to_mate(dx, g).wait_send()
        for dx in range(3):
            weight(zc, g, xsem.at[dx, g], xpeer[dx]).wait_send()


def fused(lengths, q, k, v, wt, rate, w1, w2t):
    any_spec = pl.BlockSpec(memory_space=pl.ANY)
    dma = pltpu.SemaphoreType.DMA
    return pl.pallas_call(
        fused_kernel,
        out_shape=jax.ShapeDtypeStruct((8, 192, 128), BF),
        in_specs=[
            pl.BlockSpec(memory_space=pltpu.SMEM),
            VMEM_SPEC,
            VMEM_SPEC,
            VMEM_SPEC,
            any_spec,
            VMEM_SPEC,
            VMEM_SPEC,
            VMEM_SPEC,
        ],
        out_specs=VMEM_SPEC,
        scratch_shapes=[
            pltpu.VMEM((24, 208, 128), BF),
            pltpu.VMEM((2, 64, 256), F32),
            pltpu.VMEM((32, 208, 128), BF),
            pltpu.VMEM((32, 64, 128), BF),
            dma((24,)),
            dma((32,)),
            dma((32,)),
            dma((24,)),
            pltpu.VMEM((2, 8, 2, 192, 256), BF),
            pltpu.VMEM((2, 192, 256), BF),
            pltpu.VMEM((2, 2, 576, 256), F32),
            pltpu.VMEM((2, 8, 256), F32),
            pltpu.VMEM((576, 3072), BF),
            pltpu.VMEM((576, 3072), BF),
            pltpu.VMEM((3, 8, 128), F32),
            dma,
            dma((6,)),
            dma((2,)),
            dma((4, 2, 2)),
            dma((4, 2, 2)),
            dma((8, 2, 2)),
            dma,
            dma((2,)),
            dma((2,)),
            dma((3, 2)),
            dma((4, 2)),
            dma((8, 2)),
        ]
        + SCAN_SCRATCH,
        compiler_params=pltpu.CompilerParams(
            collective_id=0, has_side_effects=True, vmem_limit_bytes=56 << 20
        ),
        name="attend_gather_scan",
    )(lengths, q, k, v, wt, rate, w1, w2t)


def body(attn_query, attn_key, attn_value, prompt_len, ttt_weight, init_w1, init_w2t, step_rate):
    def turned(array):
        return jnp.swapaxes(array, 1, 2)

    results = fused(
        jnp.swapaxes(prompt_len, 0, 1),
        turned(attn_query),
        turned(attn_key),
        turned(attn_value),
        ttt_weight.T,
        jnp.swapaxes(step_rate, 0, 1),
        init_w1,
        init_w2t,
    )
    return turned(results)


def solution(mesh):
    in_specs = (
        P(None, "seg", "head"),
        P(None, "seg", "head"),
        P(None, "seg", "head"),
        P(None, "seg"),
        P(None, "head"),
        P("head", None, None),
        P("head", None, None),
        P(None, "head", "seg"),
    )
    return jax.shard_map(
        body, mesh=mesh, in_specs=in_specs, out_specs=P(None, "seg", "head"), check_vma=False
    )
```

```python
import math

import jax
import jax.numpy as jnp
from jax import lax
from jax.experimental import pallas as pl
from jax.experimental.pallas import tpu as pltpu
from jax.sharding import PartitionSpec as P

F32, BF = jnp.float32, jnp.bfloat16
GC = math.sqrt(2.0 / math.pi)
GA = 0.044715
MESH = pl.DeviceIdType.MESH
VMEM_SPEC = pl.BlockSpec(memory_space=pltpu.VMEM)


def nn(a, b):
    return lax.dot_general(a, b, (((1,), (0,)), ((), ())), preferred_element_type=F32)


def nt(a, b):
    return lax.dot_general(a, b, (((1,), (1,)), ((), ())), preferred_element_type=F32)


def tn(a, b):
    return lax.dot_general(a, b, (((0,), (0,)), ((), ())), preferred_element_type=F32)


def attend(q, k, v, length, put):
    position = lax.broadcasted_iota(jnp.int32, (128, 1), 0)
    usable = (position >= 64) | (position < length)
    for h in range(3):
        rows = slice(64 * h, 64 * h + 64)
        scores = tn(k[rows, :], q[rows, :]) * 0.125
        scores = jnp.where(usable, scores, -1e30)
        exponent = jnp.exp(scores - jnp.max(scores, axis=0, keepdims=True))
        weights = (exponent * (1.0 / jnp.sum(exponent, axis=0, keepdims=True))).astype(BF)
        put(h, nn(v[rows, :], weights).astype(BF))


def forward(u, w2b, xt, st):
    sq = u * u
    t = jnp.tanh(u * (GC + (GC * GA) * sq))
    half = 0.5 + 0.5 * t
    hb = (u * half).astype(BF)
    z = nn(w2b, hb)
    center = z - jnp.mean(z, axis=0, keepdims=True)
    rs = lax.rsqrt(jnp.mean(center * center, axis=0, keepdims=True) + 1e-5)
    y = center * rs
    return sq, t, half, hb, rs, y, y + (xt - st)


def scan_items(get, put, ready, leave, w10, w2t0, w1s, w2s, w2ts, ub, xs, rprev, count):
    left = lax.broadcasted_iota(jnp.int32, (64, 128), 1) < 64
    left1 = lax.broadcasted_iota(jnp.int32, (1, 128), 1) < 64
    zero = jnp.zeros((64, 128), F32)
    zero1 = jnp.zeros((1, 128), F32)
    w1s[...] = w10.T
    w2s[...] = w2t0
    w2ts[...] = w2t0.T
    ready(0)
    x0 = jnp.where(left, get(0, 64, 64), zero)
    ub[...] = nn(w1s[...].astype(BF), x0.astype(BF))
    xs[...] = x0.T.astype(BF)

    def step(xt, st, eta, xnt):
        xntb = xnt.astype(BF)
        u = ub[...]
        sq, t, half, hb, rs, y, r = forward(u, w2s[...].astype(BF), xt, st)
        dy = r * (eta * (1.0 / 64.0))
        m1 = jnp.mean(dy, axis=0, keepdims=True)
        m2 = jnp.mean(dy * y, axis=0, keepdims=True)
        dzb = (rs * (dy - m1 - y * m2)).astype(BF)
        slope = half + (0.5 * u) * ((1.0 - t * t) * (GC + (3.0 * GC * GA) * sq))
        dub = (nn(w2ts[...].astype(BF), dzb) * slope).astype(BF)
        x = xs[...]
        w1 = w1s[...]
        ub[...] = nn(w1.astype(BF), xntb) - nn(dub, nn(x, xntb).astype(BF))
        w1s[...] = w1 - nn(dub, x)
        w2s[...] -= nt(dzb, hb)
        w2ts[...] -= nt(hb, dzb)
        xs[...] = xnt.T.astype(BF)
        return r

    def segment(s, carry):
        prev = jnp.maximum(s - 1, 0)

        @pl.when(s + 1 < count)
        def _():
            ready(s + 1)

        qs, ks, vs = get(s, 0, 64), get(s, 64, 64), get(s, 128, 64)
        qp = get(prev, 0, 64)
        kn = get(jnp.minimum(s + 1, count - 1), 64, 64)
        rate = get(s, 192, 1)
        mid = jnp.where(left, qs, ks)
        even = step(
            jnp.where(left, ks, qp), jnp.where(left, vs, zero), jnp.where(left1, rate, zero1), mid
        )
        put(prev, jnp.where(left, rprev[...], even).astype(BF))
        rprev[...] = step(
            mid, jnp.where(left, zero, vs), jnp.where(left1, zero1, rate), jnp.where(left, kn, qs)
        )

        @pl.when(s > 0)
        def _():
            leave(prev)

        return carry

    rprev[...] = zero
    lax.fori_loop(0, count, segment, 0)
    last = forward(ub[...], w2s[...].astype(BF), get(count - 1, 0, 64), zero)[-1]
    put(count - 1, jnp.where(left, rprev[...], last).astype(BF))


SCAN_SCRATCH = [
    pltpu.VMEM((256, 64), F32),
    pltpu.VMEM((64, 256), F32),
    pltpu.VMEM((256, 64), F32),
    pltpu.VMEM((256, 128), F32),
    pltpu.VMEM((128, 64), BF),
    pltpu.VMEM((64, 128), F32),
]


def fused_kernel(
    lengths, q, k, v, wt, rate, w1, w2t, res,
    items, wsel, qkv, outs, ssend, qsem, osem, hsem,
    buf, pbuf, acc, ssq, wv, wb, rate2,
    wsem, isem, psem, rsem, lsem, recv, csem, ysend, yrecv, xsem, qsend, qrecv, msem, wrecv, *scratch,
):
    me_h, me_s = lax.axis_index("head"), lax.axis_index("seg")
    z, y = me_h // 2, lax.rem(me_h, 2)
    row, x, core = me_s // 8, lax.rem(me_s // 2, 4), lax.rem(me_s, 2)
    other = 1 - y

    def device(seg, head):
        return {"seg": seg, "head": head}

    right, left = device(me_s, lax.rem(me_h + 2, 16)), device(me_s, lax.rem(me_h + 14, 16))
    partner = device(me_s, 2 * z + other)
    above = device(lax.rem(me_s + 8, 32), 2 * z + lax.rem(y + (row + 1) // 4, 2))
    below = device(lax.rem(me_s + 24, 32), 2 * z + lax.rem(y + (4 - row) // 4, 2))
    xpeer = [device(8 * row + 2 * lax.rem(x + dx, 4) + core, me_h) for dx in (1, 2, 3)]
    mate = device(8 * row + 2 * x + 1 - core, me_h)
    barrier = pltpu.get_barrier_semaphore()

    def greet(n, carry):
        peer = lax.rem(me_s + n, 32)
        for target in (device(peer, me_h), device(peer, 2 * z + other)):
            pl.semaphore_signal(barrier, inc=1, device_id=target, device_id_type=MESH)
        return carry

    lax.fori_loop(1, 32, greet, 0)
    for target in (right, left, partner):
        pl.semaphore_signal(barrier, inc=1, device_id=target, device_id_type=MESH)
    load = pltpu.make_async_copy(wt, wv, wsem)
    load.start()
    pl.semaphore_wait(barrier, 65)

    def remote(src, dst, send, receive, peer):
        return pltpu.make_async_remote_copy(
            src_ref=src, dst_ref=dst, send_sem=send, recv_sem=receive,
            device_id=peer, device_id_type=MESH,
        )

    me = me_s
    own = jnp.minimum(me, 23)
    borrowed = own < 12
    video, head = 4 * y + lax.rem(own, 12) // 3, lax.rem(own, 3)
    group = lax.rem(y + 1 - own // 12, 2)

    def start_weight(n):
        source = w1 if n == 0 else w2t
        return remote(source.at[head], wsel.at[n], isem.at[2 + n], isem.at[n], partner)

    def start_local(n):
        source = w1 if n == 0 else w2t
        return pltpu.make_async_copy(source.at[head], wsel.at[n], isem.at[n])

    rates = remote(rate, rate2, isem.at[4], isem.at[5], partner)
    rates.start()

    for n in range(2):

        @pl.when(borrowed)
        def _():
            start_weight(n).start()

        @pl.when(jnp.logical_not(borrowed))
        def _():
            start_local(n).start()


    def block(zo, c, yo, sem, peer):
        return remote(buf.at[c, zo, yo], buf.at[c, zo, yo], sem, recv.at[zo, c, yo], peer)

    def to_right(zo, c, yo, d, o):
        return block(zo, c, yo, rsem.at[d, o, c], right)

    def to_left(zo, c, yo, d, o):
        return block(zo, c, yo, lsem.at[d, o, c], left)

    def to_partner(c):
        return remote(pbuf.at[c], buf.at[c, z, y], psem.at[c], recv.at[z, c, y], partner)

    zc = 2 * x + core
    lanes = pl.ds(pl.multiple_of(zc * 384, 128), 384)

    def half_of(chunk, g):
        columns = pl.ds(pl.multiple_of(chunk * 384, 128), 384)
        return wb.at[pl.ds(pl.multiple_of(288 * g, 32), 288), columns]

    def cross(g, peer):
        source = wt.at[pl.ds(288 * g, 288), lanes]
        return remote(source, half_of(zc, g), csem, yrecv.at[g], peer)

    def onward(g):
        peer = device(lax.rem(me_s + 8 + 16 * g, 32), me_h)
        return remote(half_of(zc, g), half_of(zc, g), ysend.at[g], yrecv.at[g], peer)

    def weight(chunk, g, sem, peer):
        return remote(half_of(chunk, g), half_of(chunk, g), sem, wrecv.at[chunk, g], peer)

    def chunk_at(dx):
        return 2 * lax.rem(x + dx, 4) + core

    def to_mate(dx, g):
        return weight(chunk_at(dx), g, msem.at[dx, g], mate)

    def spread(g):
        weight(zc, g, xsem.at[0, g], xpeer[0]).start()
        weight(zc, g, xsem.at[1, g], xpeer[2]).start()
        to_mate(0, g).start()

    def quarter(way, g, dx=None):
        chunk = chunk_at((3, 1)[way] if dx is None else dx)
        columns = pl.ds(pl.multiple_of(chunk * 384, 128), 384)
        part = wb.at[pl.ds(pl.multiple_of(288 * g + 144 * way, 16), 144), columns]
        return remote(part, part, qsend.at[way, g], qrecv.at[way, g], xpeer[2 * way])

    def pass_on(g):
        for way, dx in ((0, 3), (1, 1)):
            weight(chunk_at(dx), g, csem, mate).wait_recv()
            quarter(way, g).start()
            to_mate(dx, g).start()

    def take_far(g):
        for way in range(2):
            quarter(way, g, 2).wait_recv()
        to_mate(2, g).start()

    sooner = row // 2
    later = 1 - sooner
    edge = (row == 0) | (row == 3)

    def attend_pair(pair, put_half):
        for half in range(2):
            video = 2 * pair + half

            def put(h, value):
                put_half(slice(64 * h, 64 * h + 64), slice(128 * half, 128 * half + 128), value)

            attend(q[video], k[video], v[video], lengths[0, video], put)

    def hop(d, o, c):
        yo = y if o == 0 else other
        zr, zl = lax.rem(z + 8 - d, 8), lax.rem(z + d, 8)
        if d < 4 or c == 0:
            to_right(zr, c, yo, 0, 0).wait_recv()
        if d < 3 or (d == 3 and c == 0):
            to_right(zr, c, yo, d, o).start()
        if d < 4 or c == 1:
            to_left(zl, c, yo, 0, 0).wait_recv()
        if d < 3 or (d == 3 and c == 1):
            to_left(zl, c, yo, d, o).start()

    def send_own(c):
        to_right(z, c, y, 0, 0).start()
        to_left(z, c, y, 0, 0).start()

    def take_partner(c):
        block(z, c, other, psem.at[c], partner).wait_recv()
        to_right(z, c, other, 0, 1).start()
        to_left(z, c, other, 0, 1).start()

    @pl.when(row == 3)
    def _():
        cross(0, above).start()

    @pl.when(row == 0)
    def _():
        cross(1, below).start()

    def attend_both(c, carry):
        def put_own(rows, cols, value):
            buf[c, z, y, rows, cols] = value

        def put_partner(rows, cols, value):
            pbuf[c, rows, cols] = value

        attend_pair(2 * y + c, put_own)

        @pl.when(c == 1)
        def _():
            to_partner(0).start()

            @pl.when(edge)
            def _():
                onward(sooner).wait_recv()
                onward(sooner).start()
                spread(sooner)

        attend_pair(2 * other + c, put_partner)
        send_own(c)
        return carry

    lax.fori_loop(0, 2, attend_both, 0)
    load.wait()
    acc[...] = jnp.zeros((2, 2, 576, 256), F32)
    to_partner(1).start()
    hop(1, 0, 0)
    hop(1, 0, 1)
    hop(2, 0, 0)

    @pl.when(jnp.logical_not(edge))
    def _():
        onward(sooner).wait_recv()
        onward(sooner).start()
        spread(sooner)

    hop(2, 0, 1)
    hop(3, 0, 0)
    take_partner(0)
    hop(3, 0, 1)

    @pl.when(jnp.logical_not(edge))
    def _():
        onward(later).wait_recv()
        onward(later).start()
        spread(later)

    hop(1, 1, 0)
    pass_on(sooner)
    take_partner(1)
    hop(2, 1, 0)

    @pl.when(edge)
    def _():
        onward(later).wait_recv()
        spread(later)

    hop(1, 1, 1)
    take_far(sooner)
    hop(3, 1, 0)
    hop(2, 1, 1)
    hop(4, 0, 0)
    hop(4, 1, 0)
    pass_on(later)

    def item_out(i):
        return pltpu.make_async_remote_copy(
            src_ref=items.at[i],
            dst_ref=qkv.at[me],
            send_sem=ssend.at[i],
            recv_sem=qsem.at[me],
            device_id={"seg": i, "head": me_h},
            device_id_type=MESH,
        )

    def item_in(s):
        return pltpu.make_async_remote_copy(
            src_ref=items.at[0],
            dst_ref=qkv.at[s],
            send_sem=ssend.at[0],
            recv_sem=qsem.at[s],
            device_id={"seg": s, "head": me_h},
            device_id_type=MESH,
        )

    def place(v, h):
        return res.at[v, pl.ds(pl.multiple_of(64 * h, 64), 64), :]

    def item_own():
        return pltpu.make_async_copy(items.at[own], qkv.at[own], qsem.at[own])

    def home(s):
        return pltpu.make_async_remote_copy(
            src_ref=outs.at[s],
            dst_ref=place(video, head),
            send_sem=osem.at[s],
            recv_sem=hsem.at[video * 3 + head],
            device_id={"seg": s, "head": 2 * z + group},
            device_id_type=MESH,
        )

    def home_own():
        return pltpu.make_async_copy(outs.at[own], place(video, head), hsem.at[video * 3 + head])

    def home_in(n):
        return pltpu.make_async_remote_copy(
            src_ref=outs.at[0],
            dst_ref=place(n // 3, lax.rem(n, 3)),
            send_sem=osem.at[0],
            recv_sem=hsem.at[n],
            device_id={"seg": me, "head": 2 * z + 1 - y},
            device_id_type=MESH,
        )

    def stays(s):
        return (s == me) & (group == y)

    position = lax.broadcasted_iota(jnp.int32, (1, 128), 1)

    def finish(g, c):
        mean = jnp.sum(ssq[c], axis=0, keepdims=True) * (1.0 / 3072.0)
        projected = (acc[g, c] * lax.rsqrt(mean + 1e-6)).astype(BF)
        source_rate = rate if g == 0 else rate2
        for half in range(2):
            at = 4 * y + 2 * c + half
            usable = (position >= 64) | (position < lengths[0, at])
            for h in range(3):
                slot = (12 if g == 0 else 0) + (2 * c + half) * 3 + h
                items[slot, 0:192, :] = projected[
                    192 * h : 192 * h + 192, 128 * half : 128 * half + 128
                ]
                eta = jnp.where(usable, source_rate[h, pl.ds(at, 1), :], 0.0)
                items[slot, 192:208, :] = jnp.broadcast_to(eta, (16, 128)).astype(BF)

    def send_items(g, c):
        def send(n, carry):
            i = (12 if g == 0 else 0) + 6 * c + lax.rem(me + n, 6)

            @pl.when(i != me)
            def _():
                item_out(i).start()

            @pl.when(i == me)
            def _():
                item_own().start()

            return carry

        lax.fori_loop(0, 6, send, 0)

    def project_own(c):
        xb = buf[c].reshape(3072, 256)
        acc[0, c] = nn(wv[...], xb)
        xf = xb.astype(F32)
        ssq[c] = jnp.sum((xf * xf).reshape(384, 8, 256), axis=0)

    def project_other(g, c):
        rows = pl.ds(pl.multiple_of(288 * g, 32), 288)
        acc[1, c, rows, :] = nn(wb[rows, :], buf[c].reshape(3072, 256))

    def from_mate(n, g):
        weight(2 * n + 1 - core, g, csem, mate).wait_recv()

    hop(3, 1, 1)
    project_own(0)
    finish(0, 0)
    take_far(later)
    send_items(0, 0)
    for n in range(4):
        from_mate(n, sooner)
    project_other(sooner, 0)
    hop(4, 0, 1)
    hop(4, 1, 1)
    project_own(1)
    finish(0, 1)
    project_other(sooner, 1)
    send_items(0, 1)
    rates.wait_recv()
    for n in range(4):
        from_mate(n, later)
    project_other(later, 0)
    finish(1, 0)
    project_other(later, 1)
    send_items(1, 0)
    finish(1, 1)


    def drain(c, carry):
        to_partner(c).wait_send()
        for o in range(2):
            for d in range(3):
                to_right(z, c, y, d, o).wait_send()
                to_left(z, c, y, d, o).wait_send()

            @pl.when(c == 0)
            def _():
                to_right(z, c, y, 3, o).wait_send()

            @pl.when(c == 1)
            def _():
                to_left(z, c, y, 3, o).wait_send()

        return carry

    lax.fori_loop(0, 2, drain, 0)
    send_items(1, 1)

    for n in range(2):

        @pl.when(borrowed)
        def _():
            start_weight(n).wait_recv()

        @pl.when(jnp.logical_not(borrowed))
        def _():
            start_local(n).wait()

    def leave_home(s):
        @pl.when(stays(s))
        def _():
            home_own().start()

        @pl.when(jnp.logical_not(stays(s)))
        def _():
            home(s).start()

    @pl.when(me < 24)
    def _():
        def get(s, row, rows):
            return qkv[s, row : row + rows, :].astype(F32)

        def put(s, value):
            outs[s] = value

        def ready(s):
            @pl.when(s == me)
            def _():
                item_own().wait()

            @pl.when(s != me)
            def _():
                item_in(s).wait_recv()

        scan_items(get, put, ready, leave_home, wsel[0], wsel[1], *scratch, 32)

    def drain_sends(i, carry):
        @pl.when(i != me)
        def _():
            item_out(i).wait_send()

        return carry

    lax.fori_loop(0, 24, drain_sends, 0)

    @pl.when(me < 24)
    def _():
        leave_home(31)

    mine = (me < 24) & (group == y)

    def drain_items(n, carry):
        local = mine & (n == video * 3 + head)

        @pl.when(local)
        def _():
            home_own().wait()

        @pl.when(jnp.logical_not(local))
        def _():
            home_in(n).wait_recv()

        return carry

    lax.fori_loop(0, 24, drain_items, 0)

    @pl.when(me < 24)
    def _():
        def drain_homes(s, carry):
            @pl.when(jnp.logical_not(stays(s)))
            def _():
                home(s).wait_send()

            return carry

        lax.fori_loop(0, 32, drain_homes, 0)

    rates.wait_send()

    for n in range(2):

        @pl.when(borrowed)
        def _():
            start_weight(n).wait_send()

    @pl.when(edge)
    def _():
        cross(0, above).wait_send()

    onward(sooner).wait_send()

    @pl.when(jnp.logical_not(edge))
    def _():
        onward(later).wait_send()

    for g in range(2):
        for dx in range(4):
            to_mate(dx, g).wait_send()
        for way in range(2):
            weight(zc, g, xsem.at[way, g], xpeer[2 * way]).wait_send()
            quarter(way, g).wait_send()


def fused(lengths, q, k, v, wt, rate, w1, w2t):
    any_spec = pl.BlockSpec(memory_space=pl.ANY)
    dma = pltpu.SemaphoreType.DMA
    return pl.pallas_call(
        fused_kernel,
        out_shape=jax.ShapeDtypeStruct((8, 192, 128), BF),
        in_specs=[
            pl.BlockSpec(memory_space=pltpu.SMEM),
            VMEM_SPEC,
            VMEM_SPEC,
            VMEM_SPEC,
            any_spec,
            VMEM_SPEC,
            VMEM_SPEC,
            VMEM_SPEC,
        ],
        out_specs=VMEM_SPEC,
        scratch_shapes=[
            pltpu.VMEM((24, 208, 128), BF),
            pltpu.VMEM((2, 64, 256), F32),
            pltpu.VMEM((32, 208, 128), BF),
            pltpu.VMEM((32, 64, 128), BF),
            dma((24,)),
            dma((32,)),
            dma((32,)),
            dma((24,)),
            pltpu.VMEM((2, 8, 2, 192, 256), BF),
            pltpu.VMEM((2, 192, 256), BF),
            pltpu.VMEM((2, 2, 576, 256), F32),
            pltpu.VMEM((2, 8, 256), F32),
            pltpu.VMEM((576, 3072), BF),
            pltpu.VMEM((576, 3072), BF),
            pltpu.VMEM((3, 8, 128), F32),
            dma,
            dma((6,)),
            dma((2,)),
            dma((4, 2, 2)),
            dma((4, 2, 2)),
            dma((8, 2, 2)),
            dma,
            dma((2,)),
            dma((2,)),
            dma((2, 2)),
            dma((2, 2)),
            dma((2, 2)),
            dma((4, 2)),
            dma((8, 2)),
        ]
        + SCAN_SCRATCH,
        compiler_params=pltpu.CompilerParams(
            collective_id=0, has_side_effects=True, vmem_limit_bytes=56 << 20
        ),
        name="attend_gather_scan",
    )(lengths, q, k, v, wt, rate, w1, w2t)


def body(attn_query, attn_key, attn_value, prompt_len, ttt_weight, init_w1, init_w2t, step_rate):
    def turned(array):
        return jnp.swapaxes(array, 1, 2)

    results = fused(
        jnp.swapaxes(prompt_len, 0, 1),
        turned(attn_query),
        turned(attn_key),
        turned(attn_value),
        ttt_weight.T,
        jnp.swapaxes(step_rate, 0, 1),
        init_w1,
        init_w2t,
    )
    return turned(results)


def solution(mesh):
    in_specs = (
        P(None, "seg", "head"),
        P(None, "seg", "head"),
        P(None, "seg", "head"),
        P(None, "seg"),
        P(None, "head"),
        P("head", None, None),
        P("head", None, None),
        P(None, "head", "seg"),
    )
    return jax.shard_map(
        body, mesh=mesh, in_specs=in_specs, out_specs=P(None, "seg", "head"), check_vma=False
    )
```

```python
import math

import jax
import jax.numpy as jnp
from jax import lax
from jax.experimental import pallas as pl
from jax.experimental.pallas import tpu as pltpu
from jax.sharding import PartitionSpec as P

F32, BF = jnp.float32, jnp.bfloat16
GC = math.sqrt(2.0 / math.pi)
GA = 0.044715
MESH = pl.DeviceIdType.MESH
VMEM_SPEC = pl.BlockSpec(memory_space=pltpu.VMEM)


def nn(a, b):
    return lax.dot_general(a, b, (((1,), (0,)), ((), ())), preferred_element_type=F32)


def nt(a, b):
    return lax.dot_general(a, b, (((1,), (1,)), ((), ())), preferred_element_type=F32)


def tn(a, b):
    return lax.dot_general(a, b, (((0,), (0,)), ((), ())), preferred_element_type=F32)


def attend(q, k, v, length, put):
    position = lax.broadcasted_iota(jnp.int32, (128, 1), 0)
    usable = (position >= 64) | (position < length)
    for h in range(3):
        rows = slice(64 * h, 64 * h + 64)
        scores = tn(k[rows, :], q[rows, :]) * 0.125
        scores = jnp.where(usable, scores, -1e30)
        exponent = jnp.exp(scores - jnp.max(scores, axis=0, keepdims=True))
        weights = (exponent * (1.0 / jnp.sum(exponent, axis=0, keepdims=True))).astype(BF)
        put(h, nn(v[rows, :], weights).astype(BF))


def forward(u, w2b, xt, st):
    sq = u * u
    t = jnp.tanh(u * (GC + (GC * GA) * sq))
    half = 0.5 + 0.5 * t
    hb = (u * half).astype(BF)
    z = nn(w2b, hb)
    center = z - jnp.mean(z, axis=0, keepdims=True)
    rs = lax.rsqrt(jnp.mean(center * center, axis=0, keepdims=True) + 1e-5)
    y = center * rs
    return sq, t, half, hb, rs, y, y + (xt - st)


def scan_items(get, put, ready, leave, w10, w2t0, w1s, w2s, w2ts, ub, xs, rprev, count):
    left = lax.broadcasted_iota(jnp.int32, (64, 128), 1) < 64
    left1 = lax.broadcasted_iota(jnp.int32, (1, 128), 1) < 64
    zero = jnp.zeros((64, 128), F32)
    zero1 = jnp.zeros((1, 128), F32)
    w1s[...] = w10.T
    w2s[...] = w2t0
    w2ts[...] = w2t0.T
    ready(0)
    x0 = jnp.where(left, get(0, 64, 64), zero)
    ub[...] = nn(w1s[...].astype(BF), x0.astype(BF))
    xs[...] = x0.T.astype(BF)

    def step(xt, st, eta, xnt):
        xntb = xnt.astype(BF)
        u = ub[...]
        sq, t, half, hb, rs, y, r = forward(u, w2s[...].astype(BF), xt, st)
        dy = r * (eta * (1.0 / 64.0))
        m1 = jnp.mean(dy, axis=0, keepdims=True)
        m2 = jnp.mean(dy * y, axis=0, keepdims=True)
        dzb = (rs * (dy - m1 - y * m2)).astype(BF)
        slope = half + (0.5 * u) * ((1.0 - t * t) * (GC + (3.0 * GC * GA) * sq))
        dub = (nn(w2ts[...].astype(BF), dzb) * slope).astype(BF)
        x = xs[...]
        w1 = w1s[...]
        ub[...] = nn(w1.astype(BF), xntb) - nn(dub, nn(x, xntb).astype(BF))
        w1s[...] = w1 - nn(dub, x)
        w2s[...] -= nt(dzb, hb)
        w2ts[...] -= nt(hb, dzb)
        xs[...] = xnt.T.astype(BF)
        return r

    def segment(s, carry):
        prev = jnp.maximum(s - 1, 0)

        @pl.when(s + 1 < count)
        def _():
            ready(s + 1)

        qs, ks, vs = get(s, 0, 64), get(s, 64, 64), get(s, 128, 64)
        qp = get(prev, 0, 64)
        kn = get(jnp.minimum(s + 1, count - 1), 64, 64)
        rate = get(s, 192, 1)
        mid = jnp.where(left, qs, ks)
        even = step(
            jnp.where(left, ks, qp), jnp.where(left, vs, zero), jnp.where(left1, rate, zero1), mid
        )
        put(prev, jnp.where(left, rprev[...], even).astype(BF))
        rprev[...] = step(
            mid, jnp.where(left, zero, vs), jnp.where(left1, zero1, rate), jnp.where(left, kn, qs)
        )

        @pl.when(s > 0)
        def _():
            leave(prev)

        return carry

    rprev[...] = zero
    lax.fori_loop(0, count, segment, 0)
    last = forward(ub[...], w2s[...].astype(BF), get(count - 1, 0, 64), zero)[-1]
    put(count - 1, jnp.where(left, rprev[...], last).astype(BF))


SCAN_SCRATCH = [
    pltpu.VMEM((256, 64), F32),
    pltpu.VMEM((64, 256), F32),
    pltpu.VMEM((256, 64), F32),
    pltpu.VMEM((256, 128), F32),
    pltpu.VMEM((128, 64), BF),
    pltpu.VMEM((64, 128), F32),
]


def fused_kernel(
    lengths, q, k, v, wt, rate, w1, w2t, res,
    items, wsel, qkv, outs, ssend, qsem, osem, hsem, go,
    buf, pbuf, acc, ssq, wv, wb, rate2,
    wsem, isem, psem, rsem, lsem, recv, csem, ysend, yrecv, xsem, msem, wrecv, *scratch,
):
    me_h, me_s = lax.axis_index("head"), lax.axis_index("seg")
    z, y = me_h // 2, lax.rem(me_h, 2)
    row, x, core = me_s // 8, lax.rem(me_s // 2, 4), lax.rem(me_s, 2)
    other = 1 - y

    def device(seg, head):
        return {"seg": seg, "head": head}

    right, left = device(me_s, lax.rem(me_h + 2, 16)), device(me_s, lax.rem(me_h + 14, 16))
    partner = device(me_s, 2 * z + other)
    above = device(lax.rem(me_s + 8, 32), 2 * z + lax.rem(y + (row + 1) // 4, 2))
    below = device(lax.rem(me_s + 24, 32), 2 * z + lax.rem(y + (4 - row) // 4, 2))
    xpeer = [device(8 * row + 2 * lax.rem(x + dx, 4) + core, me_h) for dx in (1, 2, 3)]
    mate = device(8 * row + 2 * x + 1 - core, me_h)
    barrier = pltpu.get_barrier_semaphore()

    def greet(n, carry):
        peer = lax.rem(me_s + n, 32)
        for target in (device(peer, me_h), device(peer, 2 * z + other)):
            pl.semaphore_signal(barrier, inc=1, device_id=target, device_id_type=MESH)
        return carry

    lax.fori_loop(1, 32, greet, 0)
    for target in (right, left, partner):
        pl.semaphore_signal(barrier, inc=1, device_id=target, device_id_type=MESH)
    load = pltpu.make_async_copy(wt, wv, wsem)
    load.start()
    pl.semaphore_wait(barrier, 65)

    def remote(src, dst, send, receive, peer):
        return pltpu.make_async_remote_copy(
            src_ref=src, dst_ref=dst, send_sem=send, recv_sem=receive,
            device_id=peer, device_id_type=MESH,
        )

    me = me_s
    own = jnp.minimum(me, 23)
    borrowed = own < 12
    video, head = 4 * y + lax.rem(own, 12) // 3, lax.rem(own, 3)
    group = lax.rem(y + 1 - own // 12, 2)

    def start_weight(n):
        source = w1 if n == 0 else w2t
        return remote(source.at[head], wsel.at[n], isem.at[2 + n], isem.at[n], partner)

    def start_local(n):
        source = w1 if n == 0 else w2t
        return pltpu.make_async_copy(source.at[head], wsel.at[n], isem.at[n])

    rates = remote(rate, rate2, isem.at[4], isem.at[5], partner)
    rates.start()

    for n in range(2):

        @pl.when(borrowed)
        def _():
            start_weight(n).start()

        @pl.when(jnp.logical_not(borrowed))
        def _():
            start_local(n).start()


    def block(zo, c, yo, sem, peer):
        return remote(buf.at[c, zo, yo], buf.at[c, zo, yo], sem, recv.at[zo, c, yo], peer)

    def to_right(zo, c, yo, d, o):
        return block(zo, c, yo, rsem.at[d, o, c], right)

    def to_left(zo, c, yo, d, o):
        return block(zo, c, yo, lsem.at[d, o, c], left)

    def to_partner(c):
        return remote(pbuf.at[c], buf.at[c, z, y], psem.at[c], recv.at[z, c, y], partner)

    zc = 2 * x + core
    lanes = pl.ds(pl.multiple_of(zc * 384, 128), 384)

    def half_of(chunk, g):
        columns = pl.ds(pl.multiple_of(chunk * 384, 128), 384)
        return wb.at[pl.ds(pl.multiple_of(288 * g, 32), 288), columns]

    def cross(g, peer):
        source = wt.at[pl.ds(288 * g, 288), lanes]
        return remote(source, half_of(zc, g), csem, yrecv.at[g], peer)

    def onward(g):
        peer = device(lax.rem(me_s + 8 + 16 * g, 32), me_h)
        return remote(half_of(zc, g), half_of(zc, g), ysend.at[g], yrecv.at[g], peer)

    def weight(chunk, g, sem, peer):
        return remote(half_of(chunk, g), half_of(chunk, g), sem, wrecv.at[chunk, g], peer)

    def chunk_at(dx):
        return 2 * lax.rem(x + dx, 4) + core

    def to_mate(dx, g):
        return weight(chunk_at(dx), g, msem.at[dx, g], mate)

    def spread(g):
        for dx in (1, 3, 2):
            weight(zc, g, xsem.at[dx - 1, g], xpeer[dx - 1]).start()
        to_mate(0, g).start()

    sooner = row // 2
    later = 1 - sooner
    edge = (row == 0) | (row == 3)

    def attend_pair(pair, put_half):
        for half in range(2):
            video = 2 * pair + half

            def put(h, value):
                put_half(slice(64 * h, 64 * h + 64), slice(128 * half, 128 * half + 128), value)

            attend(q[video], k[video], v[video], lengths[0, video], put)

    def hop(d, o, c):
        yo = y if o == 0 else other
        zr, zl = lax.rem(z + 8 - d, 8), lax.rem(z + d, 8)
        if d < 4 or c == 0:
            to_right(zr, c, yo, 0, 0).wait_recv()
        if d < 3 or (d == 3 and c == 0):
            to_right(zr, c, yo, d, o).start()
        if d < 4 or c == 1:
            to_left(zl, c, yo, 0, 0).wait_recv()
        if d < 3 or (d == 3 and c == 1):
            to_left(zl, c, yo, d, o).start()

    def send_own(c):
        to_right(z, c, y, 0, 0).start()
        to_left(z, c, y, 0, 0).start()

    def take_partner(c):
        block(z, c, other, psem.at[c], partner).wait_recv()
        to_right(z, c, other, 0, 1).start()
        to_left(z, c, other, 0, 1).start()

    @pl.when(row == 3)
    def _():
        cross(0, above).start()

    @pl.when(row == 0)
    def _():
        cross(1, below).start()

    def attend_partner(c, carry):
        def put_half(rows, cols, value):
            pbuf[c, rows, cols] = value

        attend_pair(2 * other + c, put_half)

        @pl.when(c == 1)
        def _():
            to_partner(0).start()

        return carry

    lax.fori_loop(0, 2, attend_partner, 0)

    def attend_own(c, carry):
        def put_half(rows, cols, value):
            buf[c, z, y, rows, cols] = value

        attend_pair(2 * y + c, put_half)

        @pl.when(c == 0)
        def _():
            to_partner(1).start()

            @pl.when(edge)
            def _():
                onward(sooner).wait_recv()
                onward(sooner).start()
                spread(sooner)

        @pl.when(c == 1)
        def _():
            send_own(0)

        return carry

    lax.fori_loop(0, 2, attend_own, 0)
    load.wait()
    acc[...] = jnp.zeros((2, 2, 576, 256), F32)
    send_own(1)
    hop(1, 0, 0)
    hop(1, 0, 1)

    @pl.when(jnp.logical_not(edge))
    def _():
        onward(sooner).wait_recv()
        onward(sooner).start()
        spread(sooner)

    hop(2, 0, 0)
    take_partner(0)
    hop(2, 0, 1)

    @pl.when(jnp.logical_not(edge))
    def _():
        onward(later).wait_recv()
        onward(later).start()
        spread(later)

    hop(3, 0, 0)
    hop(1, 1, 0)
    hop(3, 0, 1)
    take_partner(1)
    hop(2, 1, 0)

    @pl.when(edge)
    def _():
        onward(later).wait_recv()
        spread(later)

    hop(1, 1, 1)
    for dx in (1, 3, 2):
        weight(chunk_at(dx), sooner, csem, mate).wait_recv()
        to_mate(dx, sooner).start()
    hop(3, 1, 0)
    hop(2, 1, 1)
    hop(4, 0, 0)
    hop(4, 1, 0)

    def item_out(i):
        return pltpu.make_async_remote_copy(
            src_ref=items.at[i],
            dst_ref=qkv.at[me],
            send_sem=ssend.at[i],
            recv_sem=qsem.at[me],
            device_id={"seg": i, "head": me_h},
            device_id_type=MESH,
        )

    def item_in(s):
        return pltpu.make_async_remote_copy(
            src_ref=items.at[0],
            dst_ref=qkv.at[s],
            send_sem=ssend.at[0],
            recv_sem=qsem.at[s],
            device_id={"seg": s, "head": me_h},
            device_id_type=MESH,
        )

    def place(v, h):
        return res.at[v, pl.ds(pl.multiple_of(64 * h, 64), 64), :]

    def item_own():
        return pltpu.make_async_copy(items.at[own], qkv.at[own], qsem.at[own])

    def home(s):
        return pltpu.make_async_remote_copy(
            src_ref=outs.at[s],
            dst_ref=place(video, head),
            send_sem=osem.at[s],
            recv_sem=hsem.at[video * 3 + head],
            device_id={"seg": s, "head": 2 * z + group},
            device_id_type=MESH,
        )

    def home_own():
        return pltpu.make_async_copy(outs.at[own], place(video, head), hsem.at[video * 3 + head])

    def home_in(n):
        return pltpu.make_async_remote_copy(
            src_ref=outs.at[0],
            dst_ref=place(n // 3, lax.rem(n, 3)),
            send_sem=osem.at[0],
            recv_sem=hsem.at[n],
            device_id={"seg": me, "head": 2 * z + 1 - y},
            device_id_type=MESH,
        )

    def stays(s):
        return (s == me) & (group == y)

    position = lax.broadcasted_iota(jnp.int32, (1, 128), 1)

    def finish(g, c):
        mean = jnp.sum(ssq[c], axis=0, keepdims=True) * (1.0 / 3072.0)
        projected = (acc[g, c] * lax.rsqrt(mean + 1e-6)).astype(BF)
        source_rate = rate if g == 0 else rate2
        for half in range(2):
            at = 4 * y + 2 * c + half
            usable = (position >= 64) | (position < lengths[0, at])
            for h in range(3):
                slot = (12 if g == 0 else 0) + (2 * c + half) * 3 + h
                items[slot, 0:192, :] = projected[
                    192 * h : 192 * h + 192, 128 * half : 128 * half + 128
                ]
                eta = jnp.where(usable, source_rate[h, pl.ds(at, 1), :], 0.0)
                items[slot, 192:208, :] = jnp.broadcast_to(eta, (16, 128)).astype(BF)

    def send_items(g, c):
        def send(n, carry):
            i = (12 if g == 0 else 0) + 6 * c + lax.rem(me + n, 6)

            @pl.when(i != me)
            def _():
                item_out(i).start()

            @pl.when(i == me)
            def _():
                item_own().start()

            return carry

        lax.fori_loop(0, 6, send, 0)

    def project_own(c):
        xb = buf[c].reshape(3072, 256)
        acc[0, c] = nn(wv[...], xb)
        xf = xb.astype(F32)
        ssq[c] = jnp.sum((xf * xf).reshape(384, 8, 256), axis=0)

    def project_other(c):
        acc[1, c] = nn(wb[...], buf[c].reshape(3072, 256))

    project_own(0)
    finish(0, 0)
    hop(3, 1, 1)
    for dx in (1, 3, 2):
        weight(chunk_at(dx), later, csem, mate).wait_recv()
        to_mate(dx, later).start()
    send_items(0, 0)
    hop(4, 0, 1)
    hop(4, 1, 1)
    project_own(1)
    finish(0, 1)
    rates.wait_recv()
    for n in range(4):
        for g in range(2):
            weight(2 * n + 1 - core, g, csem, mate).wait_recv()
        if n == 0:
            send_items(0, 1)
    project_other(0)
    finish(1, 0)
    project_other(1)

    @pl.when(row < 2)
    def _():
        send_items(1, 0)

    finish(1, 1)


    def drain(c, carry):
        to_partner(c).wait_send()
        for o in range(2):
            for d in range(3):
                to_right(z, c, y, d, o).wait_send()
                to_left(z, c, y, d, o).wait_send()

            @pl.when(c == 0)
            def _():
                to_right(z, c, y, 3, o).wait_send()

            @pl.when(c == 1)
            def _():
                to_left(z, c, y, 3, o).wait_send()

        return carry

    lax.fori_loop(0, 2, drain, 0)

    @pl.when(row >= 2)
    def _():
        pl.semaphore_wait(go, 1)
        send_items(1, 0)

    send_items(1, 1)

    for n in range(2):

        @pl.when(borrowed)
        def _():
            start_weight(n).wait_recv()

        @pl.when(jnp.logical_not(borrowed))
        def _():
            start_local(n).wait()

    def leave_home(s):
        @pl.when(stays(s))
        def _():
            home_own().start()

        @pl.when(jnp.logical_not(stays(s)))
        def _():
            home(s).start()

    @pl.when(me < 24)
    def _():
        def get(s, row, rows):
            return qkv[s, row : row + rows, :].astype(F32)

        def put(s, value):
            outs[s] = value

        def ready(s):
            @pl.when(s == me)
            def _():
                item_own().wait()

            @pl.when(s != me)
            def _():
                item_in(s).wait_recv()

        def leave(s):
            leave_home(s)
            for rows, after in ((16, 2), (24, 8)):

                @pl.when((s == after) & (row == 0))
                def _():
                    pl.semaphore_signal(
                        go, inc=1, device_id=device(me + rows, me_h), device_id_type=MESH
                    )

        scan_items(get, put, ready, leave, wsel[0], wsel[1], *scratch, 32)

    def drain_sends(i, carry):
        @pl.when(i != me)
        def _():
            item_out(i).wait_send()

        return carry

    lax.fori_loop(0, 24, drain_sends, 0)

    @pl.when(me < 24)
    def _():
        leave_home(31)

    mine = (me < 24) & (group == y)

    def drain_items(n, carry):
        local = mine & (n == video * 3 + head)

        @pl.when(local)
        def _():
            home_own().wait()

        @pl.when(jnp.logical_not(local))
        def _():
            home_in(n).wait_recv()

        return carry

    lax.fori_loop(0, 24, drain_items, 0)

    @pl.when(me < 24)
    def _():
        def drain_homes(s, carry):
            @pl.when(jnp.logical_not(stays(s)))
            def _():
                home(s).wait_send()

            return carry

        lax.fori_loop(0, 32, drain_homes, 0)

    rates.wait_send()

    for n in range(2):

        @pl.when(borrowed)
        def _():
            start_weight(n).wait_send()

    @pl.when(edge)
    def _():
        cross(0, above).wait_send()

    onward(sooner).wait_send()

    @pl.when(jnp.logical_not(edge))
    def _():
        onward(later).wait_send()

    for g in range(2):
        for dx in range(4):
            to_mate(dx, g).wait_send()
        for dx in range(3):
            weight(zc, g, xsem.at[dx, g], xpeer[dx]).wait_send()


def fused(lengths, q, k, v, wt, rate, w1, w2t):
    any_spec = pl.BlockSpec(memory_space=pl.ANY)
    dma = pltpu.SemaphoreType.DMA
    return pl.pallas_call(
        fused_kernel,
        out_shape=jax.ShapeDtypeStruct((8, 192, 128), BF),
        in_specs=[
            pl.BlockSpec(memory_space=pltpu.SMEM),
            VMEM_SPEC,
            VMEM_SPEC,
            VMEM_SPEC,
            any_spec,
            VMEM_SPEC,
            VMEM_SPEC,
            VMEM_SPEC,
        ],
        out_specs=VMEM_SPEC,
        scratch_shapes=[
            pltpu.VMEM((24, 208, 128), BF),
            pltpu.VMEM((2, 64, 256), F32),
            pltpu.VMEM((32, 208, 128), BF),
            pltpu.VMEM((32, 64, 128), BF),
            dma((24,)),
            dma((32,)),
            dma((32,)),
            dma((24,)),
            pltpu.SemaphoreType.REGULAR,
            pltpu.VMEM((2, 8, 2, 192, 256), BF),
            pltpu.VMEM((2, 192, 256), BF),
            pltpu.VMEM((2, 2, 576, 256), F32),
            pltpu.VMEM((2, 8, 256), F32),
            pltpu.VMEM((576, 3072), BF),
            pltpu.VMEM((576, 3072), BF),
            pltpu.VMEM((3, 8, 128), F32),
            dma,
            dma((6,)),
            dma((2,)),
            dma((4, 2, 2)),
            dma((4, 2, 2)),
            dma((8, 2, 2)),
            dma,
            dma((2,)),
            dma((2,)),
            dma((3, 2)),
            dma((4, 2)),
            dma((8, 2)),
        ]
        + SCAN_SCRATCH,
        compiler_params=pltpu.CompilerParams(
            collective_id=0, has_side_effects=True, vmem_limit_bytes=56 << 20
        ),
        name="attend_gather_scan",
    )(lengths, q, k, v, wt, rate, w1, w2t)


def body(attn_query, attn_key, attn_value, prompt_len, ttt_weight, init_w1, init_w2t, step_rate):
    def turned(array):
        return jnp.swapaxes(array, 1, 2)

    results = fused(
        jnp.swapaxes(prompt_len, 0, 1),
        turned(attn_query),
        turned(attn_key),
        turned(attn_value),
        ttt_weight.T,
        jnp.swapaxes(step_rate, 0, 1),
        init_w1,
        init_w2t,
    )
    return turned(results)


def solution(mesh):
    in_specs = (
        P(None, "seg", "head"),
        P(None, "seg", "head"),
        P(None, "seg", "head"),
        P(None, "seg"),
        P(None, "head"),
        P("head", None, None),
        P("head", None, None),
        P(None, "head", "seg"),
    )
    return jax.shard_map(
        body, mesh=mesh, in_specs=in_specs, out_specs=P(None, "seg", "head"), check_vma=False
    )
```
